256 devices in a mesh: ctx: 64 (over y, x, z_lo), dp: 4 (over z_hi, core).
Axes of the slice: x: 4, y: 4, z: 8 (z_hi: 2, z_lo: 4; z = z_hi * 4 + z_lo), core: 2. Of those that a mesh axis runs over, the one named last changes fastest.
Arguments:
- query: bfloat16 [4, 8192, 512], P('dp', 'ctx'), may hold values from -6 to 6
- key_input: bfloat16 [4, 8192, 512], P('dp', 'ctx'), may hold values from -6 to 6
- value_input: bfloat16 [4, 8192, 512], P('dp', 'ctx'), may hold values from -6 to 6
- filter_taps: float32 [8192, 512], P('ctx'), may hold values from -6 to 6
- grad_output: bfloat16 [4, 8192, 512], P('dp', 'ctx'), may hold values from -6 to 6
Outputs:
- output: bfloat16 [4, 8192, 512], P('dp', 'ctx')
- grad_query: bfloat16 [4, 8192, 512], P('dp', 'ctx')
- grad_key: bfloat16 [4, 8192, 512], P('dp', 'ctx')
- grad_value: bfloat16 [4, 8192, 512], P('dp', 'ctx')
- grad_filter: float32 [8192, 512], P('ctx')
The draws below stay inside these ranges and needn't reach their ends.
All inputs are finite; a program needn't handle non-finite values.
Results may differ from the reference program's by a relative error of at most 0.0058.
Values may be sent and summed in bfloat16 or wider, within the bound.
No kernel may reach another device: no remote copies, remote signals or barrier semaphores. Data moves between devices by JAX's collectives and lax.ppermute only.
A program may use at most 64 MiB of HBM per device.

```python
import jax
import jax.numpy as jnp
from jax import lax

C = 512
FILTER_LENGTH = 8192
SEQS = 4


def draw_filter_taps(key, part):
    keys = jax.random.split(jax.random.fold_in(key, 71), 4)
    steps = jnp.arange(FILTER_LENGTH, dtype=jnp.float32)
    scales = jnp.exp(jax.random.uniform(keys[0], (C,), jnp.float32, jnp.log(30.0), jnp.log(4.0 * FILTER_LENGTH)))
    noise = jnp.clip(jax.random.normal(keys[1], (FILTER_LENGTH, C), jnp.float32), -6.0, 6.0)
    shard_positions = jax.random.randint(keys[2], (4,), 1, FILTER_LENGTH)
    twiddle_factors = jax.random.uniform(keys[3], (4, C), jnp.float32, 0.5, 0.8)
    log_decay_envelope = -steps[:, None] / scales[None, :]
    for pulse_train in range(4):
        received_block = (jnp.arange(FILTER_LENGTH, dtype=jnp.int32) >= shard_positions[pulse_train]).astype(jnp.float32)
        log_decay_envelope = log_decay_envelope + received_block[:, None] * jnp.log(twiddle_factors[pulse_train])[None, :]
    envelope = jnp.exp(log_decay_envelope)
    norming = 1.0 / jnp.sqrt(jnp.sum(envelope * envelope, axis=0))
    return noise * envelope * norming[None, :]


def levels(stream_key, shape, cuts, least, top_value):
    loudness, own = 1.0, jax.random.fold_in(stream_key, 6)
    for dim, shards_of in cuts:
        draws = jnp.exp(jax.random.uniform(jax.random.fold_in(own, dim), (shards_of,), jnp.float32, least / len(cuts), top_value / len(cuts)))
        loudness = loudness * jnp.repeat(draws, shape[dim] // shards_of).reshape([-1 if axis == dim else 1 for axis in range(len(shape))])
    return loudness


def gaussian(stream_key, shape, deviation, reach, cuts=(), held_as=jnp.bfloat16):
    array = jax.random.normal(stream_key, shape, jnp.float32) * deviation
    if len(cuts) > 0:
        array = levels(stream_key, shape, cuts, -0.22, 0.18) * array
    return jnp.clip(array, min=-reach, max=reach).astype(held_as)


def setup_inputs(seed: int = 0) -> dict:
    key_list = jax.random.split(jax.random.key(seed), 6)
    return {
        "query": gaussian(key_list[0], (SEQS, FILTER_LENGTH, C), 1.0, 6.0, ((0, 4), (1, 64))),
        "key_input": gaussian(key_list[1], (SEQS, FILTER_LENGTH, C), 1.0, 6.0, ((0, 4), (1, 64))),
        "value_input": gaussian(key_list[2], (SEQS, FILTER_LENGTH, C), 1.0, 6.0, ((0, 4), (1, 64))),
        "filter_taps": draw_filter_taps(jax.random.fold_in(key_list[5], 71), 0),
        "grad_output": gaussian(key_list[4], (SEQS, FILTER_LENGTH, C), 1.0, 6.0, ((0, 4), (1, 64))),
    }


def one_sequence(filter_spec, padded, pieces):
    query, key_input, value_input, grad_output = pieces
    length = query.shape[0]
    product = lax.optimization_barrier((key_input.astype(jnp.float32) * value_input.astype(jnp.float32)).astype(jnp.bfloat16))
    grad_mix = lax.optimization_barrier((grad_output.astype(jnp.float32) * query.astype(jnp.float32)).astype(jnp.bfloat16))
    prod_spec = jnp.fft.rfft(product.astype(jnp.float32), n=padded, axis=0)
    mix_spec = jnp.fft.rfft(grad_mix.astype(jnp.float32), n=padded, axis=0)
    mixed = jnp.fft.irfft(filter_spec * prod_spec, n=padded, axis=0)[:length]
    mixed = lax.optimization_barrier(mixed.astype(jnp.bfloat16)).astype(jnp.float32)
    output = (query.astype(jnp.float32) * mixed).astype(jnp.bfloat16)
    grad_query = (grad_output.astype(jnp.float32) * mixed).astype(jnp.bfloat16)
    grad_product = jnp.fft.irfft(mix_spec * jnp.conj(filter_spec), n=padded, axis=0)[:length]
    grad_product = lax.optimization_barrier(grad_product.astype(jnp.bfloat16)).astype(jnp.float32)
    grad_key = (grad_product * value_input.astype(jnp.float32)).astype(jnp.bfloat16)
    grad_value = (grad_product * key_input.astype(jnp.float32)).astype(jnp.bfloat16)
    grad_taps = jnp.fft.irfft(mix_spec * jnp.conj(prod_spec), n=padded, axis=0)[:length].astype(jnp.float32)
    return output, grad_query, grad_key, grad_value, grad_taps


def reference(query, key_input, value_input, filter_taps, grad_output):
    length = query.shape[1]
    padded = 2 * length
    filter_spec = jnp.fft.rfft(filter_taps, n=padded, axis=0)
    results = lax.map(lambda pieces: one_sequence(filter_spec, padded, pieces), (query, key_input, value_input, grad_output))
    output, grad_query, grad_key, grad_value, grad_taps = results
    grad_filter = jnp.sum(grad_taps, axis=0).astype(jnp.float32)
    return output, grad_query, grad_key, grad_value, grad_filter
```

```python
import functools

import jax
import jax.numpy as jnp
import ml_dtypes
import numpy as np
from jax import lax
from jax.experimental import pallas as pl
from jax.experimental.pallas import tpu as pltpu
from jax.sharding import PartitionSpec as P

BF16 = jnp.bfloat16
F32 = jnp.float32

BLOCKS = 64
LANES = 128
ROWS = 128
HALF = 64
SEQS = 4
C = 512
OWNERS = 256
OWNED = C // OWNERS
KINDS = 3
CHUNK = KINDS * OWNED
GROUP = 16
TILE = GROUP * SEQS * CHUNK


def two_terms(table):
    high = table.astype(ml_dtypes.bfloat16)
    low = (table - high.astype(np.float64)).astype(ml_dtypes.bfloat16)
    return high, low


def tables():
    k1 = np.arange(HALF)[:, None] + 0.5
    angle1 = 2.0 * np.pi * k1 * np.arange(BLOCKS)[None, :] / ROWS
    first = np.concatenate([np.cos(angle1), -np.sin(angle1)], axis=0)
    first_high, first_low = two_terms(first)
    first_signal = np.concatenate([first_high, first_low], axis=1)
    first_filter = np.concatenate([first_high, first_low, first_high, first_high], axis=1)
    angle_t = 2.0 * np.pi * k1 * np.arange(LANES)[None, :] / (ROWS * LANES)
    twist = np.concatenate([np.cos(angle_t), -np.sin(angle_t)], axis=0).astype(np.float32)
    index = np.arange(LANES)
    angle2 = 2.0 * np.pi * ((index[:, None] * index[None, :]) % LANES) / LANES
    cos2, sin2 = np.cos(angle2), np.sin(angle2)
    second = np.block([[cos2, -sin2], [sin2, cos2]])
    second_back = np.block([[cos2, sin2], [-sin2, cos2]])
    last = np.concatenate([np.cos(angle1.T), -np.sin(angle1.T)], axis=1) * (2.0 / (ROWS * LANES))
    last_high, last_low = two_terms(last)
    last_stack = np.concatenate([last_high, last_high, last_low], axis=1)
    row = np.arange(CHUNK * HALF)
    pick = np.zeros((CHUNK * HALF, KINDS * LANES))
    pick[row, (row % CHUNK // OWNED) * LANES + OWNED * (row // CHUNK) + row % OWNED] = 1.0
    line = np.arange(TILE)
    block = line // (SEQS * CHUNK)
    seq = line % (SEQS * CHUNK) // CHUNK
    kind = line % CHUNK // OWNED
    own = line % OWNED
    order = np.zeros((TILE, TILE))
    order[((kind * OWNED + own) * SEQS + seq) * GROUP + block, line] = 1.0
    return (
        pick.astype(ml_dtypes.bfloat16),
        order.astype(ml_dtypes.bfloat16),
        np.ascontiguousarray(order.T).astype(ml_dtypes.bfloat16),
        first_signal,
        first_filter,
        twist,
        np.stack(two_terms(second)),
        np.stack(two_terms(second_back)),
        last_stack,
    )


def mm(a, b, dims=((1,), (0,))):
    return lax.dot_general(a, b, (dims, ((), ())), preferred_element_type=F32)


def pack_kernel(q_ref, k_ref, v_ref, f_ref, g_ref, pick_ref, out_ref):
    term = lax.axis_index("dp")
    product = (k_ref[0].astype(F32) * v_ref[0].astype(F32)).astype(BF16)
    grad_mix = (g_ref[0].astype(F32) * q_ref[0].astype(F32)).astype(BF16)
    taps = f_ref[...]
    high = taps.astype(BF16).astype(F32)
    rest = taps - high
    middle = rest.astype(BF16).astype(F32)
    part = jnp.where(term == 0, high, jnp.where(term == 1, middle, rest - middle)).astype(BF16)
    pick = pick_ref[...]
    for b in range(C // LANES):
        cols = slice(b * LANES, (b + 1) * LANES)
        data = jnp.concatenate([product[:, cols], grad_mix[:, cols], part[:, cols]], axis=1)
        rows = mm(pick, data, ((1,), (1,)))
        out_ref[b * CHUNK * HALF : (b + 1) * CHUNK * HALF, :] = rows.astype(BF16)


def unpack_kernel(q_ref, k_ref, v_ref, g_ref, got_ref, pick_ref, o_ref, gq_ref, gk_ref, gv_ref, gf_ref):
    pick = pick_ref[...]
    for b in range(C // LANES):
        cols = slice(b * LANES, (b + 1) * LANES)
        got = got_ref[b * CHUNK * HALF : (b + 1) * CHUNK * HALF, :]
        data = mm(got, pick, ((0,), (0,)))
        mixed = data[:, :LANES]
        back = data[:, LANES : 2 * LANES]
        gf_ref[:, cols] = data[:, 2 * LANES :]
        o_ref[0, :, cols] = (q_ref[0, :, cols].astype(F32) * mixed).astype(BF16)
        gq_ref[0, :, cols] = (g_ref[0, :, cols].astype(F32) * mixed).astype(BF16)
        gk_ref[0, :, cols] = (back * v_ref[0, :, cols].astype(F32)).astype(BF16)
        gv_ref[0, :, cols] = (back * k_ref[0, :, cols].astype(F32)).astype(BF16)


def split(x):
    high = x.astype(BF16)
    low = (x - high.astype(F32)).astype(BF16)
    return high, low


def conv_kernel(
    got_ref,
    order_ref,
    back_ref,
    fs_ref,
    ff_ref,
    tw_ref,
    sec_ref,
    secb_ref,
    last_ref,
    out_ref,
    sig_ref,
    spec_ref,
    fin_ref,
):
    order = order_ref[...]
    n_sig = KINDS * OWNED * SEQS
    for h in range(2):
        lo = 2 * h * TILE
        data = jnp.concatenate([got_ref[lo : lo + TILE, :], got_ref[lo + TILE : lo + 2 * TILE, :]], axis=1)
        sorted_rows = mm(order, data).astype(BF16)
        for s in range(n_sig):
            for u in range(2):
                at = (2 * h + u) * GROUP
                sig_ref[at : at + GROUP, s * LANES : (s + 1) * LANES] = sorted_rows[
                    s * GROUP : (s + 1) * GROUP, u * LANES : (u + 1) * LANES
                ]

    def sig(s):
        return sig_ref[:, s * LANES : (s + 1) * LANES]

    wr = tw_ref[:HALF, :]
    wi = tw_ref[HALF:, :]

    def spectra(first):
        halves = []
        for u in range(2):
            ar = first[:HALF, u * LANES : (u + 1) * LANES]
            ai = first[HALF:, u * LANES : (u + 1) * LANES]
            halves.append(jnp.concatenate([ar * wr - ai * wi, ar * wi + ai * wr], axis=1))
        high, low = split(jnp.concatenate(halves, axis=0))
        return mm(high, sec_ref[0]) + mm(low, sec_ref[0]) + mm(high, sec_ref[1])

    for p in range(KINDS * OWNED * SEQS // 2 - OWNED * SEQS // 2):
        data = sig_ref[:, 2 * p * LANES : 2 * (p + 1) * LANES]
        first = mm(fs_ref[...], jnp.concatenate([data, data], axis=0))
        spec_ref[2 * p * HALF : 2 * (p + 1) * HALF, :] = spectra(first)

    base = 2 * OWNED * SEQS
    terms = [
        jnp.concatenate([sig(base + own * SEQS + term) for own in range(OWNED)], axis=1) for term in range(3)
    ]
    first = mm(ff_ref[...], jnp.concatenate([terms[0], terms[0], terms[1], terms[2]], axis=0))
    filter_spec = spectra(first)

    def inverse(pair):
        high, low = split(jnp.concatenate(pair, axis=0))
        full = mm(high, secb_ref[0]) + mm(low, secb_ref[0]) + mm(high, secb_ref[1])
        cols = []
        for u in range(2):
            br = full[u * HALF : (u + 1) * HALF, :LANES]
            bi = full[u * HALF : (u + 1) * HALF, LANES:]
            cols.append(jnp.concatenate([br * wr + bi * wi, bi * wr - br * wi], axis=0))
        high, low = split(jnp.concatenate(cols, axis=1))
        return mm(last_ref[...], jnp.concatenate([high, low, high], axis=0))

    def keep(s, values):
        values = values.astype(BF16)
        for b in range(BLOCKS // GROUP):
            fin_ref[b // 2, s * GROUP : (s + 1) * GROUP, (b % 2) * LANES : (b % 2 + 1) * LANES] = values[
                b * GROUP : (b + 1) * GROUP, :
            ]

    taps = []
    for own in range(OWNED):
        hr = filter_spec[own * HALF : (own + 1) * HALF, :LANES]
        hi = filter_spec[own * HALF : (own + 1) * HALF, LANES:]
        qr = jnp.zeros((HALF, LANES), F32)
        qi = jnp.zeros((HALF, LANES), F32)
        for half in range(SEQS // 2):
            mixed_pair, back_pair = [], []
            for u in range(2):
                s = own * SEQS + 2 * half + u
                pr = spec_ref[s * HALF : (s + 1) * HALF, :LANES]
                pi = spec_ref[s * HALF : (s + 1) * HALF, LANES:]
                z = OWNED * SEQS + s
                gr = spec_ref[z * HALF : (z + 1) * HALF, :LANES]
                gi = spec_ref[z * HALF : (z + 1) * HALF, LANES:]
                mixed_pair.append(jnp.concatenate([hr * pr - hi * pi, hr * pi + hi * pr], axis=1))
                back_pair.append(jnp.concatenate([gr * hr + gi * hi, gi * hr - gr * hi], axis=1))
                qr = qr + (gr * pr + gi * pi)
                qi = qi + (gi * pr - gr * pi)
            for kind, pair in ((0, mixed_pair), (1, back_pair)):
                res = inverse(pair)
                for u in range(2):
                    keep((kind * OWNED + own) * SEQS + 2 * half + u, res[:, u * LANES : (u + 1) * LANES])
        taps.append(jnp.concatenate([qr, qi], axis=1))
    res = inverse(taps)
    for own in range(OWNED):
        for d in range(SEQS):
            keep((2 * OWNED + own) * SEQS + d, res[:, own * LANES : (own + 1) * LANES])

    back = back_ref[...]
    for h in range(2):
        rows = mm(back, fin_ref[h]).astype(BF16)
        lo = 2 * h * TILE
        out_ref[lo : lo + TILE, :] = rows[:, :LANES]
        out_ref[lo + TILE : lo + 2 * TILE, :] = rows[:, LANES:]


def exchange(rows):
    parts = rows.reshape(OWNERS * KINDS, OWNED, LANES)
    parts = lax.all_to_all(parts, ("ctx", "dp"), split_axis=0, concat_axis=0, tiled=True)
    return parts.reshape(OWNERS * CHUNK, LANES)


def local(query, key_input, value_input, filter_taps, grad_output):
    pick, order, back, first_signal, first_filter, twist, second, second_back, last = tables()
    rows = jax.ShapeDtypeStruct((OWNERS * CHUNK, LANES), BF16)
    limit = pltpu.CompilerParams(vmem_limit_bytes=32 * 1024 * 1024)
    sent = pl.pallas_call(pack_kernel, out_shape=rows, compiler_params=limit, name="pack")(
        query, key_input, value_input, filter_taps, grad_output, pick
    )
    got = exchange(sent)
    results = pl.pallas_call(
        conv_kernel,
        out_shape=rows,
        scratch_shapes=[
            pltpu.VMEM((BLOCKS, KINDS * OWNED * SEQS * LANES), BF16),
            pltpu.VMEM((2 * OWNED * SEQS * HALF, 2 * LANES), F32),
            pltpu.VMEM((2, TILE, 2 * LANES), BF16),
        ],
        compiler_params=limit,
        name="conv",
    )(got, order, back, first_signal, first_filter, twist, second, second_back, last)
    returned = exchange(results)
    like = jax.ShapeDtypeStruct(query.shape, BF16)
    return pl.pallas_call(
        unpack_kernel,
        out_shape=(like, like, like, like, jax.ShapeDtypeStruct(filter_taps.shape, F32)),
        compiler_params=limit,
        name="unpack",
    )(query, key_input, value_input, grad_output, returned, pick)


def solution(mesh):
    shared = P("dp", "ctx", None)
    taps = P("ctx", None)
    return jax.shard_map(
        local,
        mesh=mesh,
        in_specs=(shared, shared, shared, taps, shared),
        out_specs=(shared, shared, shared, shared, taps),
        check_vma=False,
    )
```

```python
import jax
import jax.numpy as jnp
import ml_dtypes
import numpy as np
from jax import lax
from jax.experimental import pallas as pl
from jax.experimental.pallas import tpu as pltpu
from jax.sharding import PartitionSpec as P

BF16 = jnp.bfloat16
F32 = jnp.float32

BLOCKS = 64
LANES = 128
ROWS = 128
HALF = 64
SEQS = 4
C = 512
OWNERS = 256
OWNED = C // OWNERS
KINDS = 3
CHUNK = KINDS * OWNED
GROUP = 16
TILE = GROUP * SEQS * CHUNK
PACK_VMEM = (64 * 1024 - 1024) * 1024


def two_terms(table):
    high = table.astype(ml_dtypes.bfloat16)
    low = (table - high.astype(np.float64)).astype(ml_dtypes.bfloat16)
    return high, low


def tables():
    k1 = np.arange(HALF)[:, None] + 0.5
    angle1 = 2.0 * np.pi * k1 * np.arange(BLOCKS)[None, :] / ROWS
    first = np.concatenate([np.cos(angle1), -np.sin(angle1)], axis=0)
    first_high, first_low = two_terms(first)
    first_signal = np.concatenate([first_high, first_low], axis=1)
    first_filter = np.concatenate([first_high, first_low, first_high, first_high], axis=1)
    angle_t = 2.0 * np.pi * k1 * np.arange(LANES)[None, :] / (ROWS * LANES)
    twist = np.concatenate([np.cos(angle_t), -np.sin(angle_t)], axis=0).astype(np.float32)
    index = np.arange(LANES)
    angle2 = 2.0 * np.pi * ((index[:, None] * index[None, :]) % LANES) / LANES
    cos2, sin2 = np.cos(angle2), np.sin(angle2)
    second = np.block([[cos2, -sin2], [sin2, cos2]])
    second_back = np.block([[cos2, sin2], [-sin2, cos2]])
    last = np.concatenate([np.cos(angle1.T), -np.sin(angle1.T)], axis=1) * (2.0 / (ROWS * LANES))
    last_high, last_low = two_terms(last)
    last_stack = np.concatenate([last_high, last_high, last_low], axis=1)
    row = np.arange(CHUNK * HALF)
    pick = np.zeros((CHUNK * HALF, KINDS * LANES))
    pick[row, (row % CHUNK // OWNED) * LANES + OWNED * (row // CHUNK) + row % OWNED] = 1.0
    line = np.arange(TILE)
    block = line // (SEQS * CHUNK)
    seq = line % (SEQS * CHUNK) // CHUNK
    kind = line % CHUNK // OWNED
    own = line % OWNED
    order = np.zeros((TILE, TILE))
    order[((kind * OWNED + own) * SEQS + seq) * GROUP + block, line] = 1.0
    return (
        pick.astype(ml_dtypes.bfloat16),
        order.astype(ml_dtypes.bfloat16),
        np.ascontiguousarray(order.T).astype(ml_dtypes.bfloat16),
        first_signal,
        first_filter,
        twist,
        np.stack(two_terms(second)),
        np.stack(two_terms(second_back)),
        last_stack,
    )


def mm(a, b, dims=((1,), (0,))):
    return lax.dot_general(a, b, (dims, ((), ())), preferred_element_type=F32)


def pack_kernel(q_hbm, k_hbm, v_hbm, f_hbm, g_hbm, pick_hbm, out_hbm, in_ref, f_ref, pick_ref, out_ref, in_sems, pick_sem, out_sems):
    def copies(b):
        cols = slice(b * LANES, (b + 1) * LANES)
        rows = (k_hbm, v_hbm, g_hbm, q_hbm)
        found = [pltpu.make_async_copy(src.at[0, :, cols], in_ref.at[i, b], in_sems.at[i, b]) for i, src in enumerate(rows)]
        return found + [pltpu.make_async_copy(f_hbm.at[:, cols], f_ref.at[b], in_sems.at[4, b])]

    for copy in copies(0):
        copy.start()
    pick_copy = pltpu.make_async_copy(pick_hbm, pick_ref, pick_sem)
    pick_copy.start()
    for b in range(1, C // LANES):
        for copy in copies(b):
            copy.start()
    term = lax.axis_index("dp")
    sends = []
    for b in range(C // LANES):
        for copy in copies(b):
            copy.wait()
        product = (in_ref[0, b].astype(F32) * in_ref[1, b].astype(F32)).astype(BF16)
        grad_mix = (in_ref[2, b].astype(F32) * in_ref[3, b].astype(F32)).astype(BF16)
        taps = f_ref[b]
        high = taps.astype(BF16).astype(F32)
        rest = taps - high
        middle = rest.astype(BF16).astype(F32)
        part = jnp.where(term == 0, high, jnp.where(term == 1, middle, rest - middle)).astype(BF16)
        if b == 0:
            pick_copy.wait()
        rows = mm(pick_ref[...], jnp.concatenate([product, grad_mix, part], axis=1), ((1,), (1,)))
        at = pl.ds(b * CHUNK * HALF, CHUNK * HALF)
        out_ref[b] = rows.astype(BF16)
        sends.append(pltpu.make_async_copy(out_ref.at[b], out_hbm.at[at, :], out_sems.at[b]))
        sends[-1].start()
    for copy in sends:
        copy.wait()


def unpack_kernel(q_ref, k_ref, v_ref, g_ref, got_ref, pick_ref, o_hbm, gq_hbm, gk_hbm, gv_hbm, gf_hbm, rows_ref, taps_ref, sems):
    pick = pick_ref[...]
    copies = []
    for b in range(C // LANES):
        cols = slice(b * LANES, (b + 1) * LANES)
        got = got_ref[b * CHUNK * HALF : (b + 1) * CHUNK * HALF, :]
        data = mm(got, pick, ((0,), (0,)))
        mixed = data[:, :LANES]
        back = data[:, LANES : 2 * LANES]
        taps_ref[b] = data[:, 2 * LANES :]
        rows_ref[0, b] = (q_ref[0, :, cols].astype(F32) * mixed).astype(BF16)
        rows_ref[1, b] = (g_ref[0, :, cols].astype(F32) * mixed).astype(BF16)
        rows_ref[2, b] = (back * v_ref[0, :, cols].astype(F32)).astype(BF16)
        rows_ref[3, b] = (back * k_ref[0, :, cols].astype(F32)).astype(BF16)
        for i, out in enumerate((o_hbm, gq_hbm, gk_hbm, gv_hbm)):
            copies.append(pltpu.make_async_copy(rows_ref.at[i, b], out.at[0, :, cols], sems.at[i, b]))
        copies.append(pltpu.make_async_copy(taps_ref.at[b], gf_hbm.at[:, cols], sems.at[4, b]))
        for copy in copies[-5:]:
            copy.start()
    for copy in copies:
        copy.wait()


def split(x):
    high = x.astype(BF16)
    low = (x - high.astype(F32)).astype(BF16)
    return high, low


def conv_kernel(
    got_ref,
    order_ref,
    back_ref,
    fs_ref,
    ff_ref,
    tw_ref,
    sec_ref,
    secb_ref,
    last_ref,
    out_ref,
    sig_ref,
    spec_ref,
    fin_ref,
):
    order = order_ref[...]
    n_sig = KINDS * OWNED * SEQS
    for h in range(2):
        lo = 2 * h * TILE
        data = jnp.concatenate([got_ref[lo : lo + TILE, :], got_ref[lo + TILE : lo + 2 * TILE, :]], axis=1)
        sorted_rows = mm(order, data).astype(BF16)
        for s in range(n_sig):
            for u in range(2):
                at = (2 * h + u) * GROUP
                sig_ref[at : at + GROUP, s * LANES : (s + 1) * LANES] = sorted_rows[
                    s * GROUP : (s + 1) * GROUP, u * LANES : (u + 1) * LANES
                ]

    def sig(s):
        return sig_ref[:, s * LANES : (s + 1) * LANES]

    wr = tw_ref[:HALF, :]
    wi = tw_ref[HALF:, :]

    def spectra(first):
        halves = []
        for u in range(2):
            ar = first[:HALF, u * LANES : (u + 1) * LANES]
            ai = first[HALF:, u * LANES : (u + 1) * LANES]
            halves.append(jnp.concatenate([ar * wr - ai * wi, ar * wi + ai * wr], axis=1))
        high, low = split(jnp.concatenate(halves, axis=0))
        return mm(high, sec_ref[0]) + mm(low, sec_ref[0]) + mm(high, sec_ref[1])

    for p in range(KINDS * OWNED * SEQS // 2 - OWNED * SEQS // 2):
        data = sig_ref[:, 2 * p * LANES : 2 * (p + 1) * LANES]
        first = mm(fs_ref[...], jnp.concatenate([data, data], axis=0))
        spec_ref[2 * p * HALF : 2 * (p + 1) * HALF, :] = spectra(first)

    base = 2 * OWNED * SEQS
    terms = [
        jnp.concatenate([sig(base + own * SEQS + term) for own in range(OWNED)], axis=1) for term in range(3)
    ]
    first = mm(ff_ref[...], jnp.concatenate([terms[0], terms[0], terms[1], terms[2]], axis=0))
    filter_spec = spectra(first)

    def inverse(pair):
        high, low = split(jnp.concatenate(pair, axis=0))
        full = mm(high, secb_ref[0]) + mm(low, secb_ref[0]) + mm(high, secb_ref[1])
        cols = []
        for u in range(2):
            br = full[u * HALF : (u + 1) * HALF, :LANES]
            bi = full[u * HALF : (u + 1) * HALF, LANES:]
            cols.append(jnp.concatenate([br * wr + bi * wi, bi * wr - br * wi], axis=0))
        high, low = split(jnp.concatenate(cols, axis=1))
        return mm(last_ref[...], jnp.concatenate([high, low, high], axis=0))

    def keep(s, values):
        values = values.astype(BF16)
        for b in range(BLOCKS // GROUP):
            fin_ref[b // 2, s * GROUP : (s + 1) * GROUP, (b % 2) * LANES : (b % 2 + 1) * LANES] = values[
                b * GROUP : (b + 1) * GROUP, :
            ]

    taps = []
    for own in range(OWNED):
        hr = filter_spec[own * HALF : (own + 1) * HALF, :LANES]
        hi = filter_spec[own * HALF : (own + 1) * HALF, LANES:]
        qr = jnp.zeros((HALF, LANES), F32)
        qi = jnp.zeros((HALF, LANES), F32)
        for half in range(SEQS // 2):
            mixed_pair, back_pair = [], []
            for u in range(2):
                s = own * SEQS + 2 * half + u
                pr = spec_ref[s * HALF : (s + 1) * HALF, :LANES]
                pi = spec_ref[s * HALF : (s + 1) * HALF, LANES:]
                z = OWNED * SEQS + s
                gr = spec_ref[z * HALF : (z + 1) * HALF, :LANES]
                gi = spec_ref[z * HALF : (z + 1) * HALF, LANES:]
                mixed_pair.append(jnp.concatenate([hr * pr - hi * pi, hr * pi + hi * pr], axis=1))
                back_pair.append(jnp.concatenate([gr * hr + gi * hi, gi * hr - gr * hi], axis=1))
                qr = qr + (gr * pr + gi * pi)
                qi = qi + (gi * pr - gr * pi)
            for kind, pair in ((0, mixed_pair), (1, back_pair)):
                res = inverse(pair)
                for u in range(2):
                    keep((kind * OWNED + own) * SEQS + 2 * half + u, res[:, u * LANES : (u + 1) * LANES])
        taps.append(jnp.concatenate([qr, qi], axis=1))
    res = inverse(taps)
    for own in range(OWNED):
        for d in range(SEQS):
            keep((2 * OWNED + own) * SEQS + d, res[:, own * LANES : (own + 1) * LANES])

    back = back_ref[...]
    for h in range(2):
        rows = mm(back, fin_ref[h]).astype(BF16)
        lo = 2 * h * TILE
        out_ref[lo : lo + TILE, :] = rows[:, :LANES]
        out_ref[lo + TILE : lo + 2 * TILE, :] = rows[:, LANES:]


def exchange(rows):
    parts = rows.reshape(OWNERS * KINDS, OWNED, LANES)
    parts = lax.all_to_all(parts, ("ctx", "dp"), split_axis=0, concat_axis=0, tiled=True)
    return parts.reshape(OWNERS * CHUNK, LANES)


def local(query, key_input, value_input, filter_taps, grad_output):
    pick, order, back, first_signal, first_filter, twist, second, second_back, last = tables()
    rows = jax.ShapeDtypeStruct((OWNERS * CHUNK, LANES), BF16)
    limit = pltpu.CompilerParams(vmem_limit_bytes=32 * 1024 * 1024)
    hbm = pl.BlockSpec(memory_space=pltpu.HBM)
    blocks = C // LANES
    sent = pl.pallas_call(
        pack_kernel,
        out_shape=rows,
        in_specs=[hbm] * 6,
        out_specs=hbm,
        scratch_shapes=[
            pltpu.VMEM((4, blocks, LANES, LANES), BF16),
            pltpu.VMEM((blocks, LANES, LANES), F32),
            pltpu.VMEM(pick.shape, BF16),
            pltpu.VMEM((blocks, CHUNK * HALF, LANES), BF16),
            pltpu.SemaphoreType.DMA((5, blocks)),
            pltpu.SemaphoreType.DMA(()),
            pltpu.SemaphoreType.DMA((blocks,)),
        ],
        compiler_params=pltpu.CompilerParams(vmem_limit_bytes=PACK_VMEM),
        name="pack",
    )(query, key_input, value_input, filter_taps, grad_output, pick)
    got = exchange(sent)
    results = pl.pallas_call(
        conv_kernel,
        out_shape=rows,
        scratch_shapes=[
            pltpu.VMEM((BLOCKS, KINDS * OWNED * SEQS * LANES), BF16),
            pltpu.VMEM((2 * OWNED * SEQS * HALF, 2 * LANES), F32),
            pltpu.VMEM((2, TILE, 2 * LANES), BF16),
        ],
        compiler_params=limit,
        name="conv",
    )(got, order, back, first_signal, first_filter, twist, second, second_back, last)
    returned = exchange(results)
    like = jax.ShapeDtypeStruct(query.shape, BF16)
    return pl.pallas_call(
        unpack_kernel,
        out_shape=(like, like, like, like, jax.ShapeDtypeStruct(filter_taps.shape, F32)),
        out_specs=[hbm] * 5,
        scratch_shapes=[
            pltpu.VMEM((4, C // LANES, LANES, LANES), BF16),
            pltpu.VMEM((C // LANES, LANES, LANES), F32),
            pltpu.SemaphoreType.DMA((5, C // LANES)),
        ],
        compiler_params=limit,
        name="unpack",
    )(query, key_input, value_input, grad_output, returned, pick)


def solution(mesh):
    shared = P("dp", "ctx", None)
    taps = P("ctx", None)
    return jax.shard_map(
        local,
        mesh=mesh,
        in_specs=(shared, shared, shared, taps, shared),
        out_specs=(shared, shared, shared, shared, taps),
        check_vma=False,
    )
```

```python
import jax
import jax.numpy as jnp
import ml_dtypes
import numpy as np
from jax import lax
from jax.experimental import pallas as pl
from jax.experimental.pallas import tpu as pltpu
from jax.sharding import PartitionSpec as P

BF16 = jnp.bfloat16
F32 = jnp.float32

BLOCKS = 64
LANES = 128
ROWS = 128
HALF = 64
SEQS = 4
C = 512
OWNERS = 256
OWNED = C // OWNERS
KINDS = 3
CHUNK = KINDS * OWNED
GROUP = 16
TILE = GROUP * SEQS * CHUNK


def two_terms(table):
    high = table.astype(ml_dtypes.bfloat16)
    low = (table - high.astype(np.float64)).astype(ml_dtypes.bfloat16)
    return high, low


def tables():
    k1 = np.arange(HALF)[:, None] + 0.5
    angle1 = 2.0 * np.pi * k1 * np.arange(BLOCKS)[None, :] / ROWS
    first = np.concatenate([np.cos(angle1), -np.sin(angle1)], axis=0)
    first_high, first_low = two_terms(first)
    first_signal = np.concatenate([first_high, first_low], axis=1)
    first_filter = np.concatenate([first_high, first_low, first_high, first_high], axis=1)
    angle_t = 2.0 * np.pi * k1 * np.arange(LANES)[None, :] / (ROWS * LANES)
    twist = np.concatenate([np.cos(angle_t), -np.sin(angle_t)], axis=0).astype(np.float32)
    index = np.arange(LANES)
    angle2 = 2.0 * np.pi * ((index[:, None] * index[None, :]) % LANES) / LANES
    cos2, sin2 = np.cos(angle2), np.sin(angle2)
    second = np.block([[cos2, -sin2], [sin2, cos2]])
    second_back = np.block([[cos2, sin2], [-sin2, cos2]])
    last = np.concatenate([np.cos(angle1.T), -np.sin(angle1.T)], axis=1) * (2.0 / (ROWS * LANES))
    last_high, last_low = two_terms(last)
    last_stack = np.concatenate([last_high, last_high, last_low], axis=1)
    row = np.arange(CHUNK * HALF)
    pick = np.zeros((CHUNK * HALF, KINDS * LANES))
    pick[row, (row % CHUNK // OWNED) * LANES + OWNED * (row // CHUNK) + row % OWNED] = 1.0
    line = np.arange(TILE)
    block = line // (SEQS * CHUNK)
    seq = line % (SEQS * CHUNK) // CHUNK
    kind = line % CHUNK // OWNED
    own = line % OWNED
    order = np.zeros((TILE, TILE))
    order[((kind * OWNED + own) * SEQS + seq) * GROUP + block, line] = 1.0
    return (
        pick.astype(ml_dtypes.bfloat16),
        order.astype(ml_dtypes.bfloat16),
        np.ascontiguousarray(order.T).astype(ml_dtypes.bfloat16),
        first_signal,
        first_filter,
        twist,
        np.stack(two_terms(second)),
        np.stack(two_terms(second_back)),
        last_stack,
    )


def mm(a, b, dims=((1,), (0,))):
    return lax.dot_general(a, b, (dims, ((), ())), preferred_element_type=F32)


def pack_kernel(q_hbm, k_hbm, v_hbm, f_hbm, g_hbm, pick_hbm, out_ref, in_ref, f_ref, pick_ref, sems):
    copies = [pltpu.make_async_copy(src.at[0], in_ref.at[i], sems.at[i]) for i, src in enumerate((k_hbm, v_hbm, g_hbm, q_hbm))]
    copies.append(pltpu.make_async_copy(f_hbm, f_ref, sems.at[4]))
    copies.append(pltpu.make_async_copy(pick_hbm, pick_ref, sems.at[5]))
    for copy in copies:
        copy.start()
    term = lax.axis_index("dp")
    for copy in copies:
        copy.wait()
    for b in range(C // LANES):
        cols = slice(b * LANES, (b + 1) * LANES)
        product = (in_ref[0, :, cols].astype(F32) * in_ref[1, :, cols].astype(F32)).astype(BF16)
        grad_mix = (in_ref[2, :, cols].astype(F32) * in_ref[3, :, cols].astype(F32)).astype(BF16)
        taps = f_ref[:, cols]
        high = taps.astype(BF16).astype(F32)
        rest = taps - high
        middle = rest.astype(BF16).astype(F32)
        part = jnp.where(term == 0, high, jnp.where(term == 1, middle, rest - middle)).astype(BF16)
        rows = mm(pick_ref[...], jnp.concatenate([product, grad_mix, part], axis=1), ((1,), (1,)))
        out_ref[b * CHUNK * HALF : (b + 1) * CHUNK * HALF, :] = rows.astype(BF16)


def unpack_kernel(q_ref, k_ref, v_ref, g_ref, got_ref, pick_ref, o_hbm, gq_hbm, gk_hbm, gv_hbm, gf_hbm, rows_ref, taps_ref, sems):
    pick = pick_ref[...]
    copies = []
    for b in range(C // LANES):
        cols = slice(b * LANES, (b + 1) * LANES)
        got = got_ref[b * CHUNK * HALF : (b + 1) * CHUNK * HALF, :]
        data = mm(got, pick, ((0,), (0,)))
        mixed = data[:, :LANES]
        back = data[:, LANES : 2 * LANES]
        taps_ref[b] = data[:, 2 * LANES :]
        rows_ref[0, b] = (q_ref[0, :, cols].astype(F32) * mixed).astype(BF16)
        rows_ref[1, b] = (g_ref[0, :, cols].astype(F32) * mixed).astype(BF16)
        rows_ref[2, b] = (back * v_ref[0, :, cols].astype(F32)).astype(BF16)
        rows_ref[3, b] = (back * k_ref[0, :, cols].astype(F32)).astype(BF16)
        for i, out in enumerate((o_hbm, gq_hbm, gk_hbm, gv_hbm)):
            copies.append(pltpu.make_async_copy(rows_ref.at[i, b], out.at[0, :, cols], sems.at[i, b]))
        copies.append(pltpu.make_async_copy(taps_ref.at[b], gf_hbm.at[:, cols], sems.at[4, b]))
        for copy in copies[-5:]:
            copy.start()
    for copy in copies:
        copy.wait()


def split(x):
    high = x.astype(BF16)
    low = (x - high.astype(F32)).astype(BF16)
    return high, low


def conv_kernel(
    got_ref,
    order_ref,
    back_ref,
    fs_ref,
    ff_ref,
    tw_ref,
    sec_ref,
    secb_ref,
    last_ref,
    out_ref,
    sig_ref,
    spec_ref,
    fin_ref,
):
    order = order_ref[...]
    n_sig = KINDS * OWNED * SEQS
    for h in range(2):
        lo = 2 * h * TILE
        data = jnp.concatenate([got_ref[lo : lo + TILE, :], got_ref[lo + TILE : lo + 2 * TILE, :]], axis=1)
        sorted_rows = mm(order, data).astype(BF16)
        for s in range(n_sig):
            for u in range(2):
                at = (2 * h + u) * GROUP
                sig_ref[at : at + GROUP, s * LANES : (s + 1) * LANES] = sorted_rows[
                    s * GROUP : (s + 1) * GROUP, u * LANES : (u + 1) * LANES
                ]

    def sig(s):
        return sig_ref[:, s * LANES : (s + 1) * LANES]

    wr = tw_ref[:HALF, :]
    wi = tw_ref[HALF:, :]

    def spectra(first):
        halves = []
        for u in range(2):
            ar = first[:HALF, u * LANES : (u + 1) * LANES]
            ai = first[HALF:, u * LANES : (u + 1) * LANES]
            halves.append(jnp.concatenate([ar * wr - ai * wi, ar * wi + ai * wr], axis=1))
        high, low = split(jnp.concatenate(halves, axis=0))
        return mm(high, sec_ref[0]) + mm(low, sec_ref[0]) + mm(high, sec_ref[1])

    for p in range(KINDS * OWNED * SEQS // 2 - OWNED * SEQS // 2):
        data = sig_ref[:, 2 * p * LANES : 2 * (p + 1) * LANES]
        first = mm(fs_ref[...], jnp.concatenate([data, data], axis=0))
        spec_ref[2 * p * HALF : 2 * (p + 1) * HALF, :] = spectra(first)

    base = 2 * OWNED * SEQS
    terms = [
        jnp.concatenate([sig(base + own * SEQS + term) for own in range(OWNED)], axis=1) for term in range(3)
    ]
    first = mm(ff_ref[...], jnp.concatenate([terms[0], terms[0], terms[1], terms[2]], axis=0))
    filter_spec = spectra(first)

    def inverse(pair):
        high, low = split(jnp.concatenate(pair, axis=0))
        full = mm(high, secb_ref[0]) + mm(low, secb_ref[0]) + mm(high, secb_ref[1])
        cols = []
        for u in range(2):
            br = full[u * HALF : (u + 1) * HALF, :LANES]
            bi = full[u * HALF : (u + 1) * HALF, LANES:]
            cols.append(jnp.concatenate([br * wr + bi * wi, bi * wr - br * wi], axis=0))
        high, low = split(jnp.concatenate(cols, axis=1))
        return mm(last_ref[...], jnp.concatenate([high, low, high], axis=0))

    def keep(s, values):
        values = values.astype(BF16)
        for b in range(BLOCKS // GROUP):
            fin_ref[b // 2, s * GROUP : (s + 1) * GROUP, (b % 2) * LANES : (b % 2 + 1) * LANES] = values[
                b * GROUP : (b + 1) * GROUP, :
            ]

    taps = []
    for own in range(OWNED):
        hr = filter_spec[own * HALF : (own + 1) * HALF, :LANES]
        hi = filter_spec[own * HALF : (own + 1) * HALF, LANES:]
        qr = jnp.zeros((HALF, LANES), F32)
        qi = jnp.zeros((HALF, LANES), F32)
        for half in range(SEQS // 2):
            mixed_pair, back_pair = [], []
            for u in range(2):
                s = own * SEQS + 2 * half + u
                pr = spec_ref[s * HALF : (s + 1) * HALF, :LANES]
                pi = spec_ref[s * HALF : (s + 1) * HALF, LANES:]
                z = OWNED * SEQS + s
                gr = spec_ref[z * HALF : (z + 1) * HALF, :LANES]
                gi = spec_ref[z * HALF : (z + 1) * HALF, LANES:]
                mixed_pair.append(jnp.concatenate([hr * pr - hi * pi, hr * pi + hi * pr], axis=1))
                back_pair.append(jnp.concatenate([gr * hr + gi * hi, gi * hr - gr * hi], axis=1))
                qr = qr + (gr * pr + gi * pi)
                qi = qi + (gi * pr - gr * pi)
            for kind, pair in ((0, mixed_pair), (1, back_pair)):
                res = inverse(pair)
                for u in range(2):
                    keep((kind * OWNED + own) * SEQS + 2 * half + u, res[:, u * LANES : (u + 1) * LANES])
        taps.append(jnp.concatenate([qr, qi], axis=1))
    res = inverse(taps)
    for own in range(OWNED):
        for d in range(SEQS):
            keep((2 * OWNED + own) * SEQS + d, res[:, own * LANES : (own + 1) * LANES])

    back = back_ref[...]
    for h in range(2):
        rows = mm(back, fin_ref[h]).astype(BF16)
        lo = 2 * h * TILE
        out_ref[lo : lo + TILE, :] = rows[:, :LANES]
        out_ref[lo + TILE : lo + 2 * TILE, :] = rows[:, LANES:]


def exchange(rows):
    parts = rows.reshape(OWNERS * KINDS, OWNED, LANES)
    parts = lax.all_to_all(parts, ("ctx", "dp"), split_axis=0, concat_axis=0, tiled=True)
    return parts.reshape(OWNERS * CHUNK, LANES)


def local(query, key_input, value_input, filter_taps, grad_output):
    pick, order, back, first_signal, first_filter, twist, second, second_back, last = tables()
    rows = jax.ShapeDtypeStruct((OWNERS * CHUNK, LANES), BF16)
    limit = pltpu.CompilerParams(vmem_limit_bytes=32 * 1024 * 1024)
    hbm = pl.BlockSpec(memory_space=pltpu.HBM)
    inputs = (query, key_input, value_input, filter_taps, grad_output, jnp.asarray(pick))
    sent = pl.pallas_call(
        pack_kernel,
        out_shape=rows,
        in_specs=[hbm] * 6,
        scratch_shapes=[
            pltpu.VMEM((4,) + query.shape[1:], BF16),
            pltpu.VMEM(filter_taps.shape, F32),
            pltpu.VMEM(pick.shape, BF16),
            pltpu.SemaphoreType.DMA((6,)),
        ],
        compiler_params=limit,
        name="pack",
    )(*[pltpu.with_memory_space_constraint(x, pltpu.HBM) for x in inputs])
    got = exchange(sent)
    results = pl.pallas_call(
        conv_kernel,
        out_shape=rows,
        scratch_shapes=[
            pltpu.VMEM((BLOCKS, KINDS * OWNED * SEQS * LANES), BF16),
            pltpu.VMEM((2 * OWNED * SEQS * HALF, 2 * LANES), F32),
            pltpu.VMEM((2, TILE, 2 * LANES), BF16),
        ],
        compiler_params=limit,
        name="conv",
    )(got, order, back, first_signal, first_filter, twist, second, second_back, last)
    returned = exchange(results)
    like = jax.ShapeDtypeStruct(query.shape, BF16)
    return pl.pallas_call(
        unpack_kernel,
        out_shape=(like, like, like, like, jax.ShapeDtypeStruct(filter_taps.shape, F32)),
        out_specs=[hbm] * 5,
        scratch_shapes=[
            pltpu.VMEM((4, C // LANES, LANES, LANES), BF16),
            pltpu.VMEM((C // LANES, LANES, LANES), F32),
            pltpu.SemaphoreType.DMA((5, C // LANES)),
        ],
        compiler_params=limit,
        name="unpack",
    )(query, key_input, value_input, grad_output, returned, pick)


def solution(mesh):
    shared = P("dp", "ctx", None)
    taps = P("ctx", None)
    return jax.shard_map(
        local,
        mesh=mesh,
        in_specs=(shared, shared, shared, taps, shared),
        out_specs=(shared, shared, shared, shared, taps),
        check_vma=False,
    )
```

```python
import jax
import jax.numpy as jnp
import ml_dtypes
import numpy as np
from jax import lax
from jax.experimental import pallas as pl
from jax.experimental.pallas import tpu as pltpu
from jax.sharding import PartitionSpec as P

BF16 = jnp.bfloat16
F32 = jnp.float32

BLOCKS = 64
LANES = 128
ROWS = 128
HALF = 64
SEQS = 4
C = 512
CORES = 2
OWNERS = 128
OWNED = C // CORES // OWNERS
PARTS = 5
CHUNK = PARTS * OWNED
GROUP = 16
HALVES = 2
SIGNALS = HALVES * CHUNK
TILE = GROUP * SIGNALS
SWAP = ((0, 1), (1, 0))


def two_terms(table):
    high = table.astype(ml_dtypes.bfloat16)
    low = (table - high.astype(np.float64)).astype(ml_dtypes.bfloat16)
    return high, low


def tables():
    k1 = np.arange(HALF)[:, None] + 0.5
    angle1 = 2.0 * np.pi * k1 * np.arange(BLOCKS)[None, :] / ROWS
    first = np.concatenate([np.cos(angle1), -np.sin(angle1)], axis=0)
    first_high, first_low = two_terms(first)
    first_signal = np.concatenate([first_high, first_low], axis=1)
    first_filter = np.concatenate([first_high, first_low, first_high], axis=1)
    angle_t = 2.0 * np.pi * k1 * np.arange(LANES)[None, :] / (ROWS * LANES)
    twist = np.concatenate([np.cos(angle_t), -np.sin(angle_t)], axis=0).astype(np.float32)
    index = np.arange(LANES)
    angle2 = 2.0 * np.pi * ((index[:, None] * index[None, :]) % LANES) / LANES
    cos2, sin2 = np.cos(angle2), np.sin(angle2)
    second = np.block([[cos2, -sin2], [sin2, cos2]])
    second_back = np.block([[cos2, sin2], [-sin2, cos2]])
    last = np.concatenate([np.cos(angle1.T), -np.sin(angle1.T)], axis=1) * (2.0 / (ROWS * LANES))
    last_high, last_low = two_terms(last)
    last_stack = np.concatenate([last_high, last_high, last_low], axis=1)
    line = np.arange(TILE)
    block = line // SIGNALS
    half = line % SIGNALS // CHUNK
    part = line % CHUNK // OWNED
    own = line % OWNED
    seq = half * CORES + part // 3
    kind = part % 3
    slot = np.where(kind == 2, 2 * OWNED * SEQS + own * HALVES + half, (kind * OWNED + own) * SEQS + seq)
    order = np.zeros((TILE, TILE))
    order[slot * GROUP + block, line] = 1.0
    return (
        order.astype(ml_dtypes.bfloat16),
        np.ascontiguousarray(order.T).astype(ml_dtypes.bfloat16),
        first_signal,
        first_filter,
        twist,
        np.stack(two_terms(second)),
        np.stack(two_terms(second_back)),
        last_stack,
    )


def mm(a, b, dims=((1,), (0,))):
    return lax.dot_general(a, b, (dims, ((), ())), preferred_element_type=F32)


def columns(core, b):
    return pl.ds(pl.multiple_of(core * (C // CORES) + b * LANES, LANES), LANES)


def gate_kernel(q_hbm, k_hbm, v_hbm, g_hbm, out_ref, pick_ref, in_ref, sems):
    copies = [pltpu.make_async_copy(src.at[0], in_ref.at[i], sems.at[i]) for i, src in enumerate((k_hbm, v_hbm, g_hbm, q_hbm))]
    for copy in copies:
        copy.start()
    row = lax.broadcasted_iota(jnp.int32, (CHUNK * HALF, LANES), 0)
    lane = lax.broadcasted_iota(jnp.int32, (CHUNK * HALF, LANES), 1)
    first = (lane >> 1) * CHUNK + (lane & 1)
    for part in range(PARTS):
        chosen = jnp.where(row == first + OWNED * part, 1.0, 0.0)
        pick_ref[:, part * LANES : (part + 1) * LANES] = chosen.astype(BF16)
    for i in range(2):
        copies[2 * i].wait()
        copies[2 * i + 1].wait()
        out_ref[i] = (in_ref[2 * i].astype(F32) * in_ref[2 * i + 1].astype(F32)).astype(BF16)


def pack_kernel(own_ref, other_ref, f_ref, pick_ref, out_ref):
    core = lax.axis_index("core")
    term = lax.axis_index("zh")
    for b in range(C // CORES // LANES):
        cols = columns(core, b)
        taps = f_ref[:, cols]
        high = taps.astype(BF16).astype(F32)
        part = jnp.where(term == 0, high, taps - high).astype(BF16)
        data = [own_ref[0, :, cols], own_ref[1, :, cols], part, other_ref[0, :, cols], other_ref[1, :, cols]]
        rows = mm(pick_ref[...], jnp.concatenate(data, axis=1), ((1,), (1,)))
        out_ref[b * CHUNK * HALF : (b + 1) * CHUNK * HALF, :] = rows.astype(BF16)


def unpack_kernel(
    q_ref, k_ref, v_ref, g_ref, own_ref, other_ref, pick_ref, o_hbm, gq_hbm, gk_hbm, gv_hbm, gf_hbm, rows_ref, taps_ref, sems
):
    core = lax.axis_index("core")
    copies = []
    for i in range(C // LANES):
        b = i // 2
        cols = columns(core if i % 2 == 0 else 1 - core, b)
        got_ref = own_ref if i % 2 == 0 else other_ref
        got = got_ref[b * CHUNK * HALF : (b + 1) * CHUNK * HALF, :]
        if i % 2 == 0:
            data = mm(got, pick_ref[:, : 3 * LANES], ((0,), (0,)))
            mixed, back, taps = data[:, :LANES], data[:, LANES : 2 * LANES], data[:, 2 * LANES :]
        else:
            data = mm(got, pick_ref[:, 2 * LANES :], ((0,), (0,)))
            taps, mixed, back = data[:, :LANES], data[:, LANES : 2 * LANES], data[:, 2 * LANES :]
        taps_ref[i] = taps
        rows_ref[0, i] = (q_ref[0, :, cols].astype(F32) * mixed).astype(BF16)
        rows_ref[1, i] = (g_ref[0, :, cols].astype(F32) * mixed).astype(BF16)
        rows_ref[2, i] = (back * v_ref[0, :, cols].astype(F32)).astype(BF16)
        rows_ref[3, i] = (back * k_ref[0, :, cols].astype(F32)).astype(BF16)
        for j, out in enumerate((o_hbm, gq_hbm, gk_hbm, gv_hbm)):
            copies.append(pltpu.make_async_copy(rows_ref.at[j, i], out.at[0, :, cols], sems.at[j, i]))
        copies.append(pltpu.make_async_copy(taps_ref.at[i], gf_hbm.at[:, cols], sems.at[4, i]))
        for copy in copies[-5:]:
            copy.start()
    for copy in copies:
        copy.wait()


def split(x):
    high = x.astype(BF16)
    low = (x - high.astype(F32)).astype(BF16)
    return high, low


def conv_kernel(
    got_ref,
    order_ref,
    back_ref,
    fs_ref,
    ff_ref,
    tw_ref,
    sec_ref,
    secb_ref,
    last_ref,
    out_ref,
    sig_ref,
    spec_ref,
    fin_ref,
):
    order = order_ref[...]
    for h in range(2):
        lo = 2 * h * TILE
        data = jnp.concatenate([got_ref[lo : lo + TILE, :], got_ref[lo + TILE : lo + 2 * TILE, :]], axis=1)
        sorted_rows = mm(order, data).astype(BF16)
        for s in range(SIGNALS):
            for u in range(2):
                at = (2 * h + u) * GROUP
                sig_ref[at : at + GROUP, s * LANES : (s + 1) * LANES] = sorted_rows[
                    s * GROUP : (s + 1) * GROUP, u * LANES : (u + 1) * LANES
                ]

    def sig(s):
        return sig_ref[:, s * LANES : (s + 1) * LANES]

    wr = tw_ref[:HALF, :]
    wi = tw_ref[HALF:, :]

    def spectra(first):
        halves = []
        for u in range(2):
            ar = first[:HALF, u * LANES : (u + 1) * LANES]
            ai = first[HALF:, u * LANES : (u + 1) * LANES]
            halves.append(jnp.concatenate([ar * wr - ai * wi, ar * wi + ai * wr], axis=1))
        high, low = split(jnp.concatenate(halves, axis=0))
        return mm(high, sec_ref[0]) + mm(low, sec_ref[0]) + mm(high, sec_ref[1])

    for p in range(OWNED * SEQS):
        data = sig_ref[:, 2 * p * LANES : 2 * (p + 1) * LANES]
        first = mm(fs_ref[...], jnp.concatenate([data, data], axis=0))
        spec_ref[2 * p * HALF : 2 * (p + 1) * HALF, :] = spectra(first)

    base = 2 * OWNED * SEQS
    terms = [
        jnp.concatenate([sig(base + own * HALVES + term) for own in range(OWNED)], axis=1) for term in range(2)
    ]
    first = mm(ff_ref[...], jnp.concatenate([terms[0], terms[0], terms[1]], axis=0))
    filter_spec = spectra(first)

    def inverse(pair):
        high, low = split(jnp.concatenate(pair, axis=0))
        full = mm(high, secb_ref[0]) + mm(low, secb_ref[0]) + mm(high, secb_ref[1])
        cols = []
        for u in range(2):
            br = full[u * HALF : (u + 1) * HALF, :LANES]
            bi = full[u * HALF : (u + 1) * HALF, LANES:]
            cols.append(jnp.concatenate([br * wr + bi * wi, bi * wr - br * wi], axis=0))
        high, low = split(jnp.concatenate(cols, axis=1))
        return mm(last_ref[...], jnp.concatenate([high, low, high], axis=0))

    def keep(s, values):
        values = values.astype(BF16)
        for b in range(BLOCKS // GROUP):
            fin_ref[b // 2, s * GROUP : (s + 1) * GROUP, (b % 2) * LANES : (b % 2 + 1) * LANES] = values[
                b * GROUP : (b + 1) * GROUP, :
            ]

    taps = []
    for own in range(OWNED):
        hr = filter_spec[own * HALF : (own + 1) * HALF, :LANES]
        hi = filter_spec[own * HALF : (own + 1) * HALF, LANES:]
        qr = jnp.zeros((HALF, LANES), F32)
        qi = jnp.zeros((HALF, LANES), F32)
        for half in range(SEQS // 2):
            mixed_pair, back_pair = [], []
            for u in range(2):
                s = own * SEQS + 2 * half + u
                pr = spec_ref[s * HALF : (s + 1) * HALF, :LANES]
                pi = spec_ref[s * HALF : (s + 1) * HALF, LANES:]
                z = OWNED * SEQS + s
                gr = spec_ref[z * HALF : (z + 1) * HALF, :LANES]
                gi = spec_ref[z * HALF : (z + 1) * HALF, LANES:]
                mixed_pair.append(jnp.concatenate([hr * pr - hi * pi, hr * pi + hi * pr], axis=1))
                back_pair.append(jnp.concatenate([gr * hr + gi * hi, gi * hr - gr * hi], axis=1))
                qr = qr + (gr * pr + gi * pi)
                qi = qi + (gi * pr - gr * pi)
            for kind, pair in ((0, mixed_pair), (1, back_pair)):
                res = inverse(pair)
                for u in range(2):
                    keep((kind * OWNED + own) * SEQS + 2 * half + u, res[:, u * LANES : (u + 1) * LANES])
        taps.append(jnp.concatenate([qr, qi], axis=1))
    res = inverse(taps)
    for own in range(OWNED):
        for half in range(HALVES):
            keep(base + own * HALVES + half, res[:, own * LANES : (own + 1) * LANES])

    back = back_ref[...]
    for h in range(2):
        rows = mm(back, fin_ref[h]).astype(BF16)
        lo = 2 * h * TILE
        out_ref[lo : lo + TILE, :] = rows[:, :LANES]
        out_ref[lo + TILE : lo + 2 * TILE, :] = rows[:, LANES:]


def exchange(rows):
    parts = rows.reshape(OWNERS * PARTS, OWNED, LANES)
    parts = lax.all_to_all(parts, ("ctx", "zh"), split_axis=0, concat_axis=0, tiled=True)
    return parts.reshape(OWNERS * CHUNK, LANES)


def local(query, key_input, value_input, filter_taps, grad_output):
    order, back, first_signal, first_filter, twist, second, second_back, last = tables()
    rows = jax.ShapeDtypeStruct((OWNERS * CHUNK, LANES), BF16)
    limit = pltpu.CompilerParams(vmem_limit_bytes=32 * 1024 * 1024)
    hbm = pl.BlockSpec(memory_space=pltpu.HBM)
    inputs = (query, key_input, value_input, grad_output)
    gated, pick = pl.pallas_call(
        gate_kernel,
        out_shape=(
            jax.ShapeDtypeStruct((2,) + query.shape[1:], BF16),
            jax.ShapeDtypeStruct((CHUNK * HALF, PARTS * LANES), BF16),
        ),
        in_specs=[hbm] * 4,
        scratch_shapes=[pltpu.VMEM((4,) + query.shape[1:], BF16), pltpu.SemaphoreType.DMA((4,))],
        compiler_params=limit,
        name="gate",
    )(*[pltpu.with_memory_space_constraint(x, pltpu.HBM) for x in inputs])
    other = lax.ppermute(gated, "core", SWAP)
    sent = pl.pallas_call(pack_kernel, out_shape=rows, compiler_params=limit, name="pack")(gated, other, filter_taps, pick)
    got = exchange(sent)
    results = pl.pallas_call(
        conv_kernel,
        out_shape=rows,
        scratch_shapes=[
            pltpu.VMEM((BLOCKS, SIGNALS * LANES), BF16),
            pltpu.VMEM((2 * OWNED * SEQS * HALF, 2 * LANES), F32),
            pltpu.VMEM((2, TILE, 2 * LANES), BF16),
        ],
        compiler_params=limit,
        name="conv",
    )(got, order, back, first_signal, first_filter, twist, second, second_back, last)
    returned = exchange(results)
    swapped = lax.ppermute(returned, "core", SWAP)
    like = jax.ShapeDtypeStruct(query.shape, BF16)
    return pl.pallas_call(
        unpack_kernel,
        out_shape=(like, like, like, like, jax.ShapeDtypeStruct(filter_taps.shape, F32)),
        out_specs=[hbm] * 5,
        scratch_shapes=[
            pltpu.VMEM((4, C // LANES, LANES, LANES), BF16),
            pltpu.VMEM((C // LANES, LANES, LANES), F32),
            pltpu.SemaphoreType.DMA((5, C // LANES)),
        ],
        compiler_params=limit,
        name="unpack",
    )(query, key_input, value_input, grad_output, returned, swapped, pick)


def solution(mesh):
    split = jax.sharding.Mesh(mesh.devices.reshape(BLOCKS, HALVES, CORES), ("ctx", "zh", "core"))
    shared = P(("zh", "core"), "ctx", None)
    taps = P("ctx", None)
    return jax.shard_map(
        local,
        mesh=split,
        in_specs=(shared, shared, shared, taps, shared),
        out_specs=(shared, shared, shared, shared, taps),
        check_vma=False,
    )
```

```python
import functools

import jax
import jax.numpy as jnp
import ml_dtypes
import numpy as np
from jax import lax
from jax.experimental import pallas as pl
from jax.experimental.pallas import tpu as pltpu
from jax.sharding import PartitionSpec as P

BF16 = jnp.bfloat16
F32 = jnp.float32

BLOCKS = 64
LANES = 128
ROWS = 128
HALF = 64
SEQS = 4
C = 512
CORES = 2
HALVES = 2
KINDS = 3
OWNERS = 256
OWNED = C // OWNERS
GROUP = 16
IN_ROWS = KINDS * OWNED
IN_TILE = GROUP * HALVES * IN_ROWS
PARTS = 5
OUT_ROWS = PARTS * OWNED
OUT_TILE = GROUP * HALVES * OUT_ROWS
TARGETS = OWNERS // CORES
SWAP = ((0, 1), (1, 0))


def two_terms(table):
    high = table.astype(ml_dtypes.bfloat16)
    low = (table - high.astype(np.float64)).astype(ml_dtypes.bfloat16)
    return high, low


def tables():
    k1 = np.arange(HALF)[:, None] + 0.5
    angle1 = 2.0 * np.pi * k1 * np.arange(BLOCKS)[None, :] / ROWS
    first = np.concatenate([np.cos(angle1), -np.sin(angle1)], axis=0)
    first_high, first_low = two_terms(first)
    first_signal = np.concatenate([first_high, first_low], axis=1)
    first_filter = np.concatenate([first_high, first_low, first_high, first_high], axis=1)
    angle_t = 2.0 * np.pi * k1 * np.arange(LANES)[None, :] / (ROWS * LANES)
    twist = np.concatenate([np.cos(angle_t), -np.sin(angle_t)], axis=0).astype(np.float32)
    index = np.arange(LANES)
    angle2 = 2.0 * np.pi * ((index[:, None] * index[None, :]) % LANES) / LANES
    cos2, sin2 = np.cos(angle2), np.sin(angle2)
    second = np.block([[cos2, -sin2], [sin2, cos2]])
    second_back = np.block([[cos2, sin2], [-sin2, cos2]])
    last = np.concatenate([np.cos(angle1.T), -np.sin(angle1.T)], axis=1) * (2.0 / (ROWS * LANES))
    last_high, last_low = two_terms(last)
    last_stack = np.concatenate([last_high, last_high, last_low], axis=1)
    row = np.arange(IN_ROWS * HALF)
    pick = np.zeros((IN_ROWS * HALF, KINDS * LANES))
    pick[row, (row % IN_ROWS // OWNED) * LANES + OWNED * (row // IN_ROWS) + row % OWNED] = 1.0
    line = np.arange(IN_TILE)
    slot = line % IN_ROWS * HALVES + line // IN_ROWS % HALVES
    order = np.zeros((IN_TILE, IN_TILE))
    order[slot * GROUP + line // (HALVES * IN_ROWS), line] = 1.0
    line = np.arange(OUT_TILE)
    half = line % (HALVES * OUT_ROWS) // OUT_ROWS
    part = line % OUT_ROWS // OWNED
    own = line % OWNED
    slot = np.where(
        part == 4, 2 * OWNED * SEQS + own * HALVES + half, (part % 2 * OWNED + own) * SEQS + half * CORES + part // 2
    )
    back = np.zeros((OUT_TILE, OUT_TILE))
    back[line, slot * GROUP + line // (HALVES * OUT_ROWS)] = 1.0
    row = np.arange(OUT_ROWS * HALF)
    own = OWNED * (row // OUT_ROWS) + row % OWNED
    part = row % OUT_ROWS // OWNED
    sort = np.zeros((CORES, OUT_ROWS * HALF, KINDS * LANES))
    for core in range(CORES):
        for kind, wanted in enumerate((2 * core, 2 * core + 1, 4)):
            sort[core, row[part == wanted], kind * LANES + own[part == wanted]] = 1.0
    high, low = two_terms(second)
    back_high, back_low = two_terms(second_back)
    return (
        pick.astype(ml_dtypes.bfloat16),
        sort.astype(ml_dtypes.bfloat16),
        order.astype(ml_dtypes.bfloat16),
        back.astype(ml_dtypes.bfloat16),
        first_signal,
        first_filter,
        twist,
        np.concatenate([high, high, low], axis=0),
        np.concatenate([back_high, back_high, back_low], axis=0),
        last_stack,
    )


def mm(a, b, dims=((1,), (0,))):
    return lax.dot_general(a, b, (dims, ((), ())), preferred_element_type=F32)


def pack_kernel(q_hbm, k_hbm, v_hbm, f_hbm, g_hbm, pick_hbm, out_ref, in_ref, f_ref, pick_ref, sems):
    copies = [pltpu.make_async_copy(src.at[0], in_ref.at[i], sems.at[i]) for i, src in enumerate((k_hbm, v_hbm, g_hbm, q_hbm))]
    copies.append(pltpu.make_async_copy(f_hbm, f_ref, sems.at[4]))
    copies.append(pltpu.make_async_copy(pick_hbm, pick_ref, sems.at[5]))
    for copy in copies:
        copy.start()
    term = lax.axis_index("core") * HALVES + lax.axis_index("zh")
    for copy in copies:
        copy.wait()
    for b in range(C // LANES):
        cols = slice(b * LANES, (b + 1) * LANES)
        product = (in_ref[0, :, cols].astype(F32) * in_ref[1, :, cols].astype(F32)).astype(BF16)
        grad_mix = (in_ref[2, :, cols].astype(F32) * in_ref[3, :, cols].astype(F32)).astype(BF16)
        taps = f_ref[:, cols]
        high = taps.astype(BF16).astype(F32)
        rest = taps - high
        middle = rest.astype(BF16).astype(F32)
        part = jnp.where(term == 0, high, jnp.where(term == 1, middle, rest - middle)).astype(BF16)
        rows = mm(pick_ref[...], jnp.concatenate([product, grad_mix, part], axis=1), ((1,), (1,)))
        out_ref[b * IN_ROWS * HALF : (b + 1) * IN_ROWS * HALF, :] = rows.astype(BF16)


def unpack_kernel(own, q_ref, k_ref, v_ref, g_ref, got_ref, sort_ref, *refs):
    o_hbm, gq_hbm, gk_hbm, gv_hbm, gf_hbm, rows_ref, taps_ref, sems = refs[-8:]
    core = lax.axis_index("core")
    owners = core if own else 1 - core
    copies = []
    for b in range(C // CORES // LANES):
        cols = pl.ds(pl.multiple_of(owners * (C // CORES) + b * LANES, LANES), LANES)
        got = got_ref[b * OUT_ROWS * HALF : (b + 1) * OUT_ROWS * HALF, :]
        data = mm(got, sort_ref[core], ((0,), (0,)))
        mixed, back = data[:, :LANES], data[:, LANES : 2 * LANES]
        taps_ref[b] = data[:, 2 * LANES :]
        rows_ref[0, b] = (q_ref[0, :, cols].astype(F32) * mixed).astype(BF16)
        rows_ref[1, b] = (g_ref[0, :, cols].astype(F32) * mixed).astype(BF16)
        rows_ref[2, b] = (back * v_ref[0, :, cols].astype(F32)).astype(BF16)
        rows_ref[3, b] = (back * k_ref[0, :, cols].astype(F32)).astype(BF16)
        for j, out in enumerate((o_hbm, gq_hbm, gk_hbm, gv_hbm)):
            copies.append(pltpu.make_async_copy(rows_ref.at[j, b], out.at[0, :, cols], sems.at[j, b]))
        copies.append(pltpu.make_async_copy(taps_ref.at[b], gf_hbm.at[:, cols], sems.at[4, b]))
        for copy in copies[-5:]:
            copy.start()
    for copy in copies:
        copy.wait()


def split(x):
    high = x.astype(BF16)
    low = (x - high.astype(F32)).astype(BF16)
    return high, low


def conv_kernel(
    got_ref,
    order_ref,
    back_ref,
    fs_ref,
    ff_ref,
    tw_ref,
    sec_ref,
    secb_ref,
    last_ref,
    out_ref,
    sig_ref,
    spec_ref,
    inv_ref,
    fin_ref,
):
    order = order_ref[...]
    for core in range(CORES):
        for h in range(2):
            lo = (2 * core + h) * 2 * IN_TILE
            data = jnp.concatenate([got_ref[lo : lo + IN_TILE, :], got_ref[lo + IN_TILE : lo + 2 * IN_TILE, :]], axis=1)
            sorted_rows = mm(order, data).astype(BF16)
            for kind in range(KINDS):
                for own in range(OWNED):
                    for half in range(HALVES):
                        seq = core * HALVES + half if kind == 2 else half * CORES + core
                        s = (kind * OWNED + own) * SEQS + seq
                        line = ((kind * OWNED + own) * HALVES + half) * GROUP
                        for u in range(2):
                            at = (2 * h + u) * GROUP
                            sig_ref[at : at + GROUP, s * LANES : (s + 1) * LANES] = sorted_rows[
                                line : line + GROUP, u * LANES : (u + 1) * LANES
                            ]

    def sig(s):
        return sig_ref[:, s * LANES : (s + 1) * LANES]

    wr = tw_ref[:HALF, :]
    wi = tw_ref[HALF:, :]

    def three(x):
        high, low = split(x)
        return jnp.concatenate([high, low, high], axis=1)

    def turned(first):
        halves = []
        for u in range(2):
            ar = first[:HALF, u * LANES : (u + 1) * LANES]
            ai = first[HALF:, u * LANES : (u + 1) * LANES]
            halves.append(jnp.concatenate([ar * wr - ai * wi, ar * wi + ai * wr], axis=1))
        return three(jnp.concatenate(halves, axis=0))

    base = 2 * OWNED * SEQS
    lines = []
    for p in range(OWNED * SEQS):
        data = sig_ref[:, 2 * p * LANES : 2 * (p + 1) * LANES]
        lines.append(turned(mm(fs_ref[...], jnp.concatenate([data, data], axis=0))))
    terms = [jnp.concatenate([sig(base + own * SEQS + term) for own in range(OWNED)], axis=1) for term in range(3)]
    lines.append(turned(mm(ff_ref[...], jnp.concatenate([terms[0], terms[0], terms[1], terms[2]], axis=0))))
    spec_ref[...] = mm(jnp.concatenate(lines, axis=0), sec_ref[...])

    def inverse(full):
        cols = []
        for u in range(2):
            br = full[u * HALF : (u + 1) * HALF, :LANES]
            bi = full[u * HALF : (u + 1) * HALF, LANES:]
            cols.append(jnp.concatenate([br * wr + bi * wi, bi * wr - br * wi], axis=0))
        high, low = split(jnp.concatenate(cols, axis=1))
        return mm(last_ref[...], jnp.concatenate([high, low, high], axis=0))

    def keep(s, values):
        values = values.astype(BF16)
        for b in range(BLOCKS // GROUP):
            fin_ref[b // 2, s * GROUP : (s + 1) * GROUP, (b % 2) * LANES : (b % 2 + 1) * LANES] = values[
                b * GROUP : (b + 1) * GROUP, :
            ]

    taps, lines, places = [], [], []
    for own in range(OWNED):
        at = (base + own) * HALF
        hr = spec_ref[at : at + HALF, :LANES]
        hi = spec_ref[at : at + HALF, LANES:]
        qr = jnp.zeros((HALF, LANES), F32)
        qi = jnp.zeros((HALF, LANES), F32)
        for half in range(HALVES):
            mixed_pair, back_pair = [], []
            for u in range(CORES):
                s = own * SEQS + half * CORES + u
                pr = spec_ref[s * HALF : (s + 1) * HALF, :LANES]
                pi = spec_ref[s * HALF : (s + 1) * HALF, LANES:]
                z = OWNED * SEQS + s
                gr = spec_ref[z * HALF : (z + 1) * HALF, :LANES]
                gi = spec_ref[z * HALF : (z + 1) * HALF, LANES:]
                mixed_pair.append(jnp.concatenate([hr * pr - hi * pi, hr * pi + hi * pr], axis=1))
                back_pair.append(jnp.concatenate([gr * hr + gi * hi, gi * hr - gr * hi], axis=1))
                qr = qr + (gr * pr + gi * pi)
                qi = qi + (gi * pr - gr * pi)
            for kind, pair in ((0, mixed_pair), (1, back_pair)):
                lines.append(three(jnp.concatenate(pair, axis=0)))
                s = (kind * OWNED + own) * SEQS + half * CORES
                places.append([(s,), (s + 1,)])
        taps.append(jnp.concatenate([qr, qi], axis=1))
    lines.append(three(jnp.concatenate(taps, axis=0)))
    places.append([[base + own * HALVES + half for half in range(HALVES)] for own in range(OWNED)])
    inv_ref[...] = mm(jnp.concatenate(lines, axis=0), secb_ref[...])
    for p, pair in enumerate(places):
        res = inverse(inv_ref[2 * p * HALF : 2 * (p + 1) * HALF, :])
        for u in range(2):
            for s in pair[u]:
                keep(s, res[:, u * LANES : (u + 1) * LANES])

    back = back_ref[...]
    for h in range(2):
        rows = mm(back, fin_ref[h]).astype(BF16)
        lo = 2 * h * OUT_TILE
        out_ref[lo : lo + OUT_TILE, :] = rows[:, :LANES]
        out_ref[lo + OUT_TILE : lo + 2 * OUT_TILE, :] = rows[:, LANES:]


def exchange(rows, axes):
    parts = rows.reshape(rows.shape[0] // OWNED, OWNED, LANES)
    parts = lax.all_to_all(parts, axes, split_axis=0, concat_axis=0, tiled=True)
    return parts.reshape(rows.shape)


def local(query, key_input, value_input, filter_taps, grad_output):
    pick, sort, order, back, first_signal, first_filter, twist, second, second_back, last = tables()
    limit = pltpu.CompilerParams(vmem_limit_bytes=32 * 1024 * 1024)
    hbm = pl.BlockSpec(memory_space=pltpu.HBM)
    inputs = (query, key_input, value_input, filter_taps, grad_output, jnp.asarray(pick))
    sent = pl.pallas_call(
        pack_kernel,
        out_shape=jax.ShapeDtypeStruct((OWNERS * IN_ROWS, LANES), BF16),
        in_specs=[hbm] * 6,
        scratch_shapes=[
            pltpu.VMEM((4,) + query.shape[1:], BF16),
            pltpu.VMEM(filter_taps.shape, F32),
            pltpu.VMEM(pick.shape, BF16),
            pltpu.SemaphoreType.DMA((6,)),
        ],
        compiler_params=limit,
        name="pack",
    )(*[pltpu.with_memory_space_constraint(x, pltpu.HBM) for x in inputs])
    got = exchange(sent, ("core", "ctx", "zh"))
    signals = (KINDS - 1) * OWNED * SEQS + OWNED
    results = pl.pallas_call(
        conv_kernel,
        out_shape=jax.ShapeDtypeStruct((TARGETS * OUT_ROWS, LANES), BF16),
        scratch_shapes=[
            pltpu.VMEM((BLOCKS, KINDS * OWNED * SEQS * LANES), BF16),
            pltpu.VMEM((signals * HALF, 2 * LANES), F32),
            pltpu.VMEM((signals * HALF, 2 * LANES), F32),
            pltpu.VMEM((2, OUT_TILE, 2 * LANES), BF16),
        ],
        compiler_params=limit,
        name="conv",
    )(got, order, back, first_signal, first_filter, twist, second, second_back, last)
    returned = exchange(results, ("ctx", "zh"))
    swapped = lax.ppermute(returned, "core", SWAP)
    like = jax.ShapeDtypeStruct(query.shape, BF16)
    unpack = functools.partial(
        pl.pallas_call,
        out_shape=(like, like, like, like, jax.ShapeDtypeStruct(filter_taps.shape, F32)),
        out_specs=[hbm] * 5,
        scratch_shapes=[
            pltpu.VMEM((4, C // CORES // LANES, LANES, LANES), BF16),
            pltpu.VMEM((C // CORES // LANES, LANES, LANES), F32),
            pltpu.SemaphoreType.DMA((5, C // CORES // LANES)),
        ],
        compiler_params=limit,
        cost_estimate=pl.CostEstimate(flops=10**9, bytes_accessed=2 * 10**6, transcendentals=0),
    )
    near = (query, key_input, value_input, grad_output)
    half = unpack(functools.partial(unpack_kernel, True), name="unpack_own")(*near, returned, sort)
    block = pl.BlockSpec(memory_space=pltpu.VMEM)
    return unpack(
        functools.partial(unpack_kernel, False),
        in_specs=[block] * 6 + [hbm] * 5,
        input_output_aliases={6 + i: i for i in range(5)},
        name="unpack_other",
    )(*near, swapped, sort, *half)


def solution(mesh):
    split = jax.sharding.Mesh(mesh.devices.reshape(BLOCKS, HALVES, CORES), ("ctx", "zh", "core"))
    shared = P(("zh", "core"), "ctx", None)
    taps = P("ctx", None)
    return jax.shard_map(
        local,
        mesh=split,
        in_specs=(shared, shared, shared, taps, shared),
        out_specs=(shared, shared, shared, shared, taps),
        check_vma=False,
    )
```

```python
import functools

import jax
import jax.numpy as jnp
import ml_dtypes
import numpy as np
from jax import lax
from jax.experimental import pallas as pl
from jax.experimental.pallas import tpu as pltpu
from jax.sharding import PartitionSpec as P

BF16 = jnp.bfloat16
F32 = jnp.float32

BLOCKS = 64
LANES = 128
ROWS = 128
HALF = 64
SEQS = 4
C = 512
CORES = 2
HALVES = 2
KINDS = 3
OWNERS = 128
OWNED = C // CORES // OWNERS
GROUP = 16
PARTS = 5
CHUNK = PARTS * OWNED
TILE = GROUP * HALVES * CHUNK
SWAP = ((0, 1), (1, 0))


def two_terms(table):
    high = table.astype(ml_dtypes.bfloat16)
    low = (table - high.astype(np.float64)).astype(ml_dtypes.bfloat16)
    return high, low


def tables():
    k1 = np.arange(HALF)[:, None] + 0.5
    angle1 = 2.0 * np.pi * k1 * np.arange(BLOCKS)[None, :] / ROWS
    first = np.concatenate([np.cos(angle1), -np.sin(angle1)], axis=0)
    first_high, first_low = two_terms(first)
    first_signal = np.concatenate([first_high, first_low], axis=1)
    first_filter = np.concatenate([first_high, first_low, first_high], axis=1)
    angle_t = 2.0 * np.pi * k1 * np.arange(LANES)[None, :] / (ROWS * LANES)
    twist = np.concatenate([np.cos(angle_t), -np.sin(angle_t)], axis=0).astype(np.float32)
    index = np.arange(LANES)
    angle2 = 2.0 * np.pi * ((index[:, None] * index[None, :]) % LANES) / LANES
    cos2, sin2 = np.cos(angle2), np.sin(angle2)
    second = np.block([[cos2, -sin2], [sin2, cos2]])
    second_back = np.block([[cos2, sin2], [-sin2, cos2]])
    last = np.concatenate([np.cos(angle1.T), -np.sin(angle1.T)], axis=1) * (2.0 / (ROWS * LANES))
    last_high, last_low = two_terms(last)
    last_stack = np.concatenate([last_high, last_high, last_low], axis=1)
    line = np.arange(TILE)
    half = line % (HALVES * CHUNK) // CHUNK
    part = line % CHUNK // OWNED
    own = line % OWNED
    slot = np.where(
        part == 4, 2 * OWNED * SEQS + own * HALVES + half, (part % 2 * OWNED + own) * SEQS + half * CORES + part // 2
    )
    order = np.zeros((TILE, TILE))
    order[slot * GROUP + line // (HALVES * CHUNK), line] = 1.0
    row = np.arange(CHUNK * HALF)
    own = OWNED * (row // CHUNK) + row % OWNED
    part = row % CHUNK // OWNED
    sort = np.zeros((CORES, CHUNK * HALF, KINDS * LANES))
    for whose in range(CORES):
        for kind, wanted in enumerate((2 * whose, 2 * whose + 1, 4)):
            sort[whose, row[part == wanted], kind * LANES + own[part == wanted]] = 1.0
    high, low = two_terms(second)
    back_high, back_low = two_terms(second_back)
    return (
        sort.astype(ml_dtypes.bfloat16),
        order.astype(ml_dtypes.bfloat16),
        np.ascontiguousarray(order.T).astype(ml_dtypes.bfloat16),
        first_signal,
        first_filter,
        twist,
        np.concatenate([high, high, low], axis=0),
        np.concatenate([back_high, back_high, back_low], axis=0),
        last_stack,
    )


def mm(a, b, dims=((1,), (0,))):
    return lax.dot_general(a, b, (dims, ((), ())), preferred_element_type=F32)


def columns(core, b):
    return pl.ds(pl.multiple_of(core * (C // CORES) + b * LANES, LANES), LANES)


def gate_kernel(q_hbm, k_hbm, v_hbm, g_hbm, out_ref, pick_ref, in_ref, sems):
    copies = [pltpu.make_async_copy(src.at[0], in_ref.at[i], sems.at[i]) for i, src in enumerate((k_hbm, v_hbm, g_hbm, q_hbm))]
    for copy in copies:
        copy.start()
    row = lax.broadcasted_iota(jnp.int32, (CHUNK * HALF, LANES), 0)
    lane = lax.broadcasted_iota(jnp.int32, (CHUNK * HALF, LANES), 1)
    first = (lane >> 1) * CHUNK + (lane & 1)
    for part in range(PARTS):
        chosen = jnp.where(row == first + OWNED * part, 1.0, 0.0)
        pick_ref[:, part * LANES : (part + 1) * LANES] = chosen.astype(BF16)
    for i in range(2):
        copies[2 * i].wait()
        copies[2 * i + 1].wait()
        out_ref[i] = (in_ref[2 * i].astype(F32) * in_ref[2 * i + 1].astype(F32)).astype(BF16)


def pack_kernel(gated_ref, q_ref, k_ref, v_ref, g_ref, f_ref, pick_ref, out_ref):
    core = lax.axis_index("core")
    term = lax.axis_index("zh")
    for b in range(C // CORES // LANES):
        cols = columns(core, b)
        product = (k_ref[0, :, cols].astype(F32) * v_ref[0, :, cols].astype(F32)).astype(BF16)
        grad_mix = (g_ref[0, :, cols].astype(F32) * q_ref[0, :, cols].astype(F32)).astype(BF16)
        taps = f_ref[:, cols]
        high = taps.astype(BF16).astype(F32)
        part = jnp.where(term == 0, high, taps - high).astype(BF16)
        data = [gated_ref[0, :, cols], gated_ref[1, :, cols], product, grad_mix, part]
        rows = mm(pick_ref[...], jnp.concatenate(data, axis=1), ((1,), (1,)))
        out_ref[b * CHUNK * HALF : (b + 1) * CHUNK * HALF, :] = rows.astype(BF16)


def unpack_kernel(own, q_ref, k_ref, v_ref, g_ref, got_ref, sort_ref, *refs):
    o_hbm, gq_hbm, gk_hbm, gv_hbm, gf_hbm, rows_ref, taps_ref, sems = refs[-8:]
    core = lax.axis_index("core")
    owners = core if own else 1 - core
    copies = []
    for b in range(C // CORES // LANES):
        cols = columns(owners, b)
        got = got_ref[b * CHUNK * HALF : (b + 1) * CHUNK * HALF, :]
        data = mm(got, sort_ref[0 if own else 1], ((0,), (0,)))
        mixed, back = data[:, :LANES], data[:, LANES : 2 * LANES]
        taps_ref[b] = data[:, 2 * LANES :]
        rows_ref[0, b] = (q_ref[0, :, cols].astype(F32) * mixed).astype(BF16)
        rows_ref[1, b] = (g_ref[0, :, cols].astype(F32) * mixed).astype(BF16)
        rows_ref[2, b] = (back * v_ref[0, :, cols].astype(F32)).astype(BF16)
        rows_ref[3, b] = (back * k_ref[0, :, cols].astype(F32)).astype(BF16)
        for j, out in enumerate((o_hbm, gq_hbm, gk_hbm, gv_hbm)):
            copies.append(pltpu.make_async_copy(rows_ref.at[j, b], out.at[0, :, cols], sems.at[j, b]))
        copies.append(pltpu.make_async_copy(taps_ref.at[b], gf_hbm.at[:, cols], sems.at[4, b]))
        for copy in copies[-5:]:
            copy.start()
    for copy in copies:
        copy.wait()


def split(x):
    high = x.astype(BF16)
    low = (x - high.astype(F32)).astype(BF16)
    return high, low


def conv_kernel(
    got_ref,
    order_ref,
    back_ref,
    fs_ref,
    ff_ref,
    tw_ref,
    sec_ref,
    secb_ref,
    last_ref,
    out_ref,
    sig_ref,
    spec_ref,
    inv_ref,
    fin_ref,
):
    order = order_ref[...]
    for h in range(2):
        lo = 2 * h * TILE
        data = jnp.concatenate([got_ref[lo : lo + TILE, :], got_ref[lo + TILE : lo + 2 * TILE, :]], axis=1)
        sorted_rows = mm(order, data).astype(BF16)
        for s in range(HALVES * CHUNK):
            for u in range(2):
                at = (2 * h + u) * GROUP
                sig_ref[at : at + GROUP, s * LANES : (s + 1) * LANES] = sorted_rows[
                    s * GROUP : (s + 1) * GROUP, u * LANES : (u + 1) * LANES
                ]

    def sig(s):
        return sig_ref[:, s * LANES : (s + 1) * LANES]

    wr = tw_ref[:HALF, :]
    wi = tw_ref[HALF:, :]

    def three(x):
        high, low = split(x)
        return jnp.concatenate([high, low, high], axis=1)

    def turned(first):
        halves = []
        for u in range(2):
            ar = first[:HALF, u * LANES : (u + 1) * LANES]
            ai = first[HALF:, u * LANES : (u + 1) * LANES]
            halves.append(jnp.concatenate([ar * wr - ai * wi, ar * wi + ai * wr], axis=1))
        return three(jnp.concatenate(halves, axis=0))

    base = 2 * OWNED * SEQS
    lines = []
    for p in range(OWNED * SEQS):
        data = sig_ref[:, 2 * p * LANES : 2 * (p + 1) * LANES]
        lines.append(turned(mm(fs_ref[...], jnp.concatenate([data, data], axis=0))))
    terms = [jnp.concatenate([sig(base + own * HALVES + term) for own in range(OWNED)], axis=1) for term in range(2)]
    lines.append(turned(mm(ff_ref[...], jnp.concatenate([terms[0], terms[0], terms[1]], axis=0))))
    spec_ref[...] = mm(jnp.concatenate(lines, axis=0), sec_ref[...])

    def inverse(full):
        cols = []
        for u in range(2):
            br = full[u * HALF : (u + 1) * HALF, :LANES]
            bi = full[u * HALF : (u + 1) * HALF, LANES:]
            cols.append(jnp.concatenate([br * wr + bi * wi, bi * wr - br * wi], axis=0))
        high, low = split(jnp.concatenate(cols, axis=1))
        return mm(last_ref[...], jnp.concatenate([high, low, high], axis=0))

    def keep(s, values):
        values = values.astype(BF16)
        for b in range(BLOCKS // GROUP):
            fin_ref[b // 2, s * GROUP : (s + 1) * GROUP, (b % 2) * LANES : (b % 2 + 1) * LANES] = values[
                b * GROUP : (b + 1) * GROUP, :
            ]

    taps, lines, places = [], [], []
    for own in range(OWNED):
        at = (base + own) * HALF
        hr = spec_ref[at : at + HALF, :LANES]
        hi = spec_ref[at : at + HALF, LANES:]
        qr = jnp.zeros((HALF, LANES), F32)
        qi = jnp.zeros((HALF, LANES), F32)
        for half in range(HALVES):
            mixed_pair, back_pair = [], []
            for u in range(CORES):
                s = own * SEQS + half * CORES + u
                pr = spec_ref[s * HALF : (s + 1) * HALF, :LANES]
                pi = spec_ref[s * HALF : (s + 1) * HALF, LANES:]
                z = OWNED * SEQS + s
                gr = spec_ref[z * HALF : (z + 1) * HALF, :LANES]
                gi = spec_ref[z * HALF : (z + 1) * HALF, LANES:]
                mixed_pair.append(jnp.concatenate([hr * pr - hi * pi, hr * pi + hi * pr], axis=1))
                back_pair.append(jnp.concatenate([gr * hr + gi * hi, gi * hr - gr * hi], axis=1))
                qr = qr + (gr * pr + gi * pi)
                qi = qi + (gi * pr - gr * pi)
            for kind, pair in ((0, mixed_pair), (1, back_pair)):
                lines.append(three(jnp.concatenate(pair, axis=0)))
                s = (kind * OWNED + own) * SEQS + half * CORES
                places.append([(s,), (s + 1,)])
        taps.append(jnp.concatenate([qr, qi], axis=1))
    lines.append(three(jnp.concatenate(taps, axis=0)))
    places.append([[base + own * HALVES + half for half in range(HALVES)] for own in range(OWNED)])
    inv_ref[...] = mm(jnp.concatenate(lines, axis=0), secb_ref[...])
    for p, pair in enumerate(places):
        res = inverse(inv_ref[2 * p * HALF : 2 * (p + 1) * HALF, :])
        for u in range(2):
            for s in pair[u]:
                keep(s, res[:, u * LANES : (u + 1) * LANES])

    back = back_ref[...]
    for h in range(2):
        rows = mm(back, fin_ref[h]).astype(BF16)
        lo = 2 * h * TILE
        out_ref[lo : lo + TILE, :] = rows[:, :LANES]
        out_ref[lo + TILE : lo + 2 * TILE, :] = rows[:, LANES:]


def exchange(rows):
    parts = rows.reshape(rows.shape[0] // OWNED, OWNED, LANES)
    parts = lax.all_to_all(parts, ("ctx", "zh"), split_axis=0, concat_axis=0, tiled=True)
    return parts.reshape(rows.shape)


def local(query, key_input, value_input, filter_taps, grad_output):
    sort, order, back, first_signal, first_filter, twist, second, second_back, last = tables()
    limit = pltpu.CompilerParams(vmem_limit_bytes=32 * 1024 * 1024)
    hbm = pl.BlockSpec(memory_space=pltpu.HBM)
    near = (query, key_input, value_input, grad_output)
    other = [lax.ppermute(x, "core", SWAP) for x in near]
    rows = jax.ShapeDtypeStruct((OWNERS * CHUNK, LANES), BF16)
    gated, pick = pl.pallas_call(
        gate_kernel,
        out_shape=(
            jax.ShapeDtypeStruct((2,) + query.shape[1:], BF16),
            jax.ShapeDtypeStruct((CHUNK * HALF, PARTS * LANES), BF16),
        ),
        in_specs=[hbm] * 4,
        scratch_shapes=[pltpu.VMEM((4,) + query.shape[1:], BF16), pltpu.SemaphoreType.DMA((4,))],
        compiler_params=limit,
        cost_estimate=pl.CostEstimate(flops=10**9, bytes_accessed=2 * 10**6, transcendentals=0),
        name="gate",
    )(*[pltpu.with_memory_space_constraint(x, pltpu.HBM) for x in near])
    sent = pl.pallas_call(pack_kernel, out_shape=rows, compiler_params=limit, name="pack")(gated, *other, filter_taps, pick)
    got = exchange(sent)
    signals = (KINDS - 1) * OWNED * SEQS + OWNED
    results = pl.pallas_call(
        conv_kernel,
        out_shape=rows,
        scratch_shapes=[
            pltpu.VMEM((BLOCKS, HALVES * CHUNK * LANES), BF16),
            pltpu.VMEM((signals * HALF, 2 * LANES), F32),
            pltpu.VMEM((signals * HALF, 2 * LANES), F32),
            pltpu.VMEM((2, TILE, 2 * LANES), BF16),
        ],
        compiler_params=limit,
        name="conv",
    )(got, order, back, first_signal, first_filter, twist, second, second_back, last)
    returned = exchange(results)
    swapped = lax.ppermute(returned, "core", SWAP)
    like = jax.ShapeDtypeStruct(query.shape, BF16)
    unpack = functools.partial(
        pl.pallas_call,
        out_shape=(like, like, like, like, jax.ShapeDtypeStruct(filter_taps.shape, F32)),
        out_specs=[hbm] * 5,
        scratch_shapes=[
            pltpu.VMEM((4, C // CORES // LANES, LANES, LANES), BF16),
            pltpu.VMEM((C // CORES // LANES, LANES, LANES), F32),
            pltpu.SemaphoreType.DMA((5, C // CORES // LANES)),
        ],
        compiler_params=limit,
        cost_estimate=pl.CostEstimate(flops=10**9, bytes_accessed=2 * 10**6, transcendentals=0),
    )
    half = unpack(functools.partial(unpack_kernel, True), name="unpack_own")(*near, returned, sort)
    block = pl.BlockSpec(memory_space=pltpu.VMEM)
    return unpack(
        functools.partial(unpack_kernel, False),
        in_specs=[block] * 6 + [hbm] * 5,
        input_output_aliases={6 + i: i for i in range(5)},
        name="unpack_other",
    )(*near, swapped, sort, *half)


def solution(mesh):
    split = jax.sharding.Mesh(mesh.devices.reshape(BLOCKS, HALVES, CORES), ("ctx", "zh", "core"))
    shared = P(("zh", "core"), "ctx", None)
    taps = P("ctx", None)
    return jax.shard_map(
        local,
        mesh=split,
        in_specs=(shared, shared, shared, taps, shared),
        out_specs=(shared, shared, shared, shared, taps),
        check_vma=False,
    )
```

```python
import functools

import jax
import jax.numpy as jnp
import ml_dtypes
import numpy as np
from jax import lax
from jax.experimental import pallas as pl
from jax.experimental.pallas import tpu as pltpu
from jax.sharding import PartitionSpec as P

BF16 = jnp.bfloat16
F32 = jnp.float32

BLOCKS = 64
LANES = 128
ROWS = 128
HALF = 64
SEQS = 4
C = 512
CORES = 2
HALVES = 2
KINDS = 3
OWNERS = 128
OWNED = C // CORES // OWNERS
GROUP = 16
PARTS = 5
CHUNK = PARTS * OWNED
TILE = GROUP * HALVES * CHUNK
SETS = 2 * OWNED * HALVES
SWAP = ((0, 1), (1, 0))


def two_terms(table):
    high = table.astype(ml_dtypes.bfloat16)
    low = (table - high.astype(np.float64)).astype(ml_dtypes.bfloat16)
    return high, low


def tables():
    k1 = np.arange(HALF)[:, None] + 0.5
    angle1 = 2.0 * np.pi * k1 * np.arange(BLOCKS)[None, :] / ROWS
    first = np.concatenate([np.cos(angle1), -np.sin(angle1)], axis=0)
    first_high, first_low = two_terms(first)
    first_signal = np.concatenate([first_high, first_low], axis=1)
    first_filter = np.concatenate([first_high, first_low, first_high], axis=1)
    angle_t = 2.0 * np.pi * k1 * np.arange(LANES)[None, :] / (ROWS * LANES)
    twist = np.concatenate([np.cos(angle_t), -np.sin(angle_t)], axis=0).astype(np.float32)
    index = np.arange(LANES)
    angle2 = 2.0 * np.pi * ((index[:, None] * index[None, :]) % LANES) / LANES
    cos2, sin2 = np.cos(angle2), np.sin(angle2)
    second = np.block([[cos2, -sin2], [sin2, cos2]])
    second_back = np.block([[cos2, sin2], [-sin2, cos2]])
    last = np.concatenate([np.cos(angle1.T), -np.sin(angle1.T)], axis=1) * (2.0 / (ROWS * LANES))
    last_high, last_low = two_terms(last)
    last_stack = np.concatenate([last_high, last_high, last_low], axis=1)
    line = np.arange(TILE)
    block = line // (HALVES * CHUNK)
    half = line % (HALVES * CHUNK) // CHUNK
    part = line % CHUNK // OWNED
    own = line % OWNED
    slot = ((part % 2 * OWNED + own) * HALVES + half) * GROUP + block
    last_slot = (own * HALVES + half) * GROUP + block
    order_own = np.zeros((SETS * GROUP + OWNED * HALVES * GROUP, TILE))
    order_other = np.zeros((SETS * GROUP, TILE))
    order_own[slot[part < 2], line[part < 2]] = 1.0
    order_own[SETS * GROUP + last_slot[part == 4], line[part == 4]] = 1.0
    chosen = (part == 2) | (part == 3)
    order_other[slot[chosen], line[chosen]] = 1.0
    back = np.zeros((TILE, TILE))
    back[line, np.where(part == 4, 2 * SETS * GROUP + last_slot, part // 2 * SETS * GROUP + slot)] = 1.0
    row = np.arange(CHUNK * HALF)
    own = OWNED * (row // CHUNK) + row % OWNED
    part = row % CHUNK // OWNED
    sort = np.zeros((CORES, CHUNK * HALF, KINDS * LANES))
    for whose in range(CORES):
        for kind, wanted in enumerate((2 * whose, 2 * whose + 1, 4)):
            sort[whose, row[part == wanted], kind * LANES + own[part == wanted]] = 1.0
    high, low = two_terms(second)
    back_high, back_low = two_terms(second_back)
    return (
        sort.astype(ml_dtypes.bfloat16),
        order_own.astype(ml_dtypes.bfloat16),
        order_other.astype(ml_dtypes.bfloat16),
        back.astype(ml_dtypes.bfloat16),
        first_signal,
        first_filter,
        twist,
        np.concatenate([high, high, low], axis=0),
        np.concatenate([back_high, back_high, back_low], axis=0),
        last_stack,
    )


def mm(a, b, dims=((1,), (0,))):
    return lax.dot_general(a, b, (dims, ((), ())), preferred_element_type=F32)


def columns(core, b):
    return pl.ds(pl.multiple_of(core * (C // CORES) + b * LANES, LANES), LANES)


def pack_kernel(q_hbm, k_hbm, v_hbm, f_hbm, g_hbm, out_ref, in_ref, f_ref, pick_ref, sems):
    copies = [pltpu.make_async_copy(src.at[0], in_ref.at[i], sems.at[i]) for i, src in enumerate((k_hbm, v_hbm, g_hbm, q_hbm))]
    copies.append(pltpu.make_async_copy(f_hbm, f_ref, sems.at[4]))
    for copy in copies:
        copy.start()
    core = lax.axis_index("core")
    term = lax.axis_index("zh")
    row = lax.broadcasted_iota(jnp.int32, (CHUNK * HALF, LANES), 0)
    lane = lax.broadcasted_iota(jnp.int32, (CHUNK * HALF, LANES), 1)
    first = (lane >> 1) * CHUNK + (lane & 1)
    for part in range(PARTS):
        chosen = jnp.where(row == first + OWNED * part, 1.0, 0.0)
        pick_ref[:, part * LANES : (part + 1) * LANES] = chosen.astype(BF16)
    for copy in copies:
        copy.wait()
    for b in range(C // CORES // LANES):
        data = []
        for owners in (core, 1 - core):
            cols = columns(owners, b)
            for i in (0, 2):
                data.append((in_ref[i, :, cols].astype(F32) * in_ref[i + 1, :, cols].astype(F32)).astype(BF16))
        taps = f_ref[:, columns(core, b)]
        high = taps.astype(BF16).astype(F32)
        data.append(jnp.where(term == 0, high, taps - high).astype(BF16))
        rows = mm(pick_ref[...], jnp.concatenate(data, axis=1), ((1,), (1,)))
        out_ref[b * CHUNK * HALF : (b + 1) * CHUNK * HALF, :] = rows.astype(BF16)


def unpack_kernel(own, q_ref, k_ref, v_ref, g_ref, got_ref, sort_ref, *refs):
    o_hbm, gq_hbm, gk_hbm, gv_hbm, gf_hbm, rows_ref, taps_ref, sems = refs[-8:]
    core = lax.axis_index("core")
    owners = core if own else 1 - core
    copies = []
    for b in range(C // CORES // LANES):
        cols = columns(owners, b)
        got = got_ref[b * CHUNK * HALF : (b + 1) * CHUNK * HALF, :]
        data = mm(got, sort_ref[0 if own else 1], ((0,), (0,)))
        mixed, back = data[:, :LANES], data[:, LANES : 2 * LANES]
        taps_ref[b] = data[:, 2 * LANES :]
        rows_ref[0, b] = (q_ref[0, :, cols].astype(F32) * mixed).astype(BF16)
        rows_ref[1, b] = (g_ref[0, :, cols].astype(F32) * mixed).astype(BF16)
        rows_ref[2, b] = (back * v_ref[0, :, cols].astype(F32)).astype(BF16)
        rows_ref[3, b] = (back * k_ref[0, :, cols].astype(F32)).astype(BF16)
        for j, out in enumerate((o_hbm, gq_hbm, gk_hbm, gv_hbm)):
            copies.append(pltpu.make_async_copy(rows_ref.at[j, b], out.at[0, :, cols], sems.at[j, b]))
        copies.append(pltpu.make_async_copy(taps_ref.at[b], gf_hbm.at[:, cols], sems.at[4, b]))
        for copy in copies[-5:]:
            copy.start()
    for copy in copies:
        copy.wait()


def split(x):
    high = x.astype(BF16)
    low = (x - high.astype(F32)).astype(BF16)
    return high, low


def three(x):
    high, low = split(x)
    return jnp.concatenate([high, low, high], axis=1)


def sort_signals(got_ref, order_ref, sig_ref):
    order = order_ref[...]
    for h in range(2):
        lo = 2 * h * TILE
        data = jnp.concatenate([got_ref[lo : lo + TILE, :], got_ref[lo + TILE : lo + 2 * TILE, :]], axis=1)
        sorted_rows = mm(order, data).astype(BF16)
        for s in range(order.shape[0] // GROUP):
            for u in range(2):
                at = (2 * h + u) * GROUP
                sig_ref[at : at + GROUP, s * LANES : (s + 1) * LANES] = sorted_rows[
                    s * GROUP : (s + 1) * GROUP, u * LANES : (u + 1) * LANES
                ]


def turned(first, tw_ref):
    wr, wi = tw_ref[:HALF, :], tw_ref[HALF:, :]
    halves = []
    for u in range(2):
        ar = first[:HALF, u * LANES : (u + 1) * LANES]
        ai = first[HALF:, u * LANES : (u + 1) * LANES]
        halves.append(jnp.concatenate([ar * wr - ai * wi, ar * wi + ai * wr], axis=1))
    return three(jnp.concatenate(halves, axis=0))


def forward_lines(sig_ref, fs_ref, tw_ref):
    lines = []
    for p in range(SETS // 2):
        data = sig_ref[:, 2 * p * LANES : 2 * (p + 1) * LANES]
        lines.append(turned(mm(fs_ref[...], jnp.concatenate([data, data], axis=0)), tw_ref))
    return lines


def multiplied(spec_ref, filter_ref, at, sums):
    lines = []
    for own in range(OWNED):
        hr = filter_ref[at + own * HALF : at + (own + 1) * HALF, :LANES]
        hi = filter_ref[at + own * HALF : at + (own + 1) * HALF, LANES:]
        mixed_pair, back_pair = [], []
        qr, qi = sums[own]
        for half in range(HALVES):
            s = own * HALVES + half
            z = OWNED * HALVES + s
            pr = spec_ref[s * HALF : (s + 1) * HALF, :LANES]
            pi = spec_ref[s * HALF : (s + 1) * HALF, LANES:]
            gr = spec_ref[z * HALF : (z + 1) * HALF, :LANES]
            gi = spec_ref[z * HALF : (z + 1) * HALF, LANES:]
            mixed_pair.append(jnp.concatenate([hr * pr - hi * pi, hr * pi + hi * pr], axis=1))
            back_pair.append(jnp.concatenate([gr * hr + gi * hi, gi * hr - gr * hi], axis=1))
            qr = qr + (gr * pr + gi * pi)
            qi = qi + (gi * pr - gr * pi)
        sums[own] = (qr, qi)
        lines.append((own, three(jnp.concatenate(mixed_pair, axis=0))))
        lines.append((OWNED + own, three(jnp.concatenate(back_pair, axis=0))))
    return [line for _, line in sorted(lines, key=lambda entry: entry[0])]


def inverse(full, tw_ref, last_ref):
    wr, wi = tw_ref[:HALF, :], tw_ref[HALF:, :]
    cols = []
    for u in range(2):
        br = full[u * HALF : (u + 1) * HALF, :LANES]
        bi = full[u * HALF : (u + 1) * HALF, LANES:]
        cols.append(jnp.concatenate([br * wr + bi * wi, bi * wr - br * wi], axis=0))
    high, low = split(jnp.concatenate(cols, axis=1))
    return mm(last_ref[...], jnp.concatenate([high, low, high], axis=0))


def keep(fin_ref, s, values):
    values = values.astype(BF16)
    for b in range(BLOCKS // GROUP):
        fin_ref[b // 2, s * GROUP : (s + 1) * GROUP, (b % 2) * LANES : (b % 2 + 1) * LANES] = values[
            b * GROUP : (b + 1) * GROUP, :
        ]


def conv_own_kernel(
    got_ref, order_ref, fs_ref, ff_ref, tw_ref, sec_ref, secb_ref, last_ref, filter_ref, sum_ref, fin_ref, sig_ref, spec_ref, inv_ref
):
    sort_signals(got_ref, order_ref, sig_ref)
    lines = forward_lines(sig_ref, fs_ref, tw_ref)
    terms = []
    for term in range(HALVES):
        places = [SETS * LANES + (own * HALVES + term) * LANES for own in range(OWNED)]
        terms.append(jnp.concatenate([sig_ref[:, at : at + LANES] for at in places], axis=1))
    lines.append(turned(mm(ff_ref[...], jnp.concatenate([terms[0], terms[0], terms[1]], axis=0)), tw_ref))
    spec_ref[...] = mm(jnp.concatenate(lines, axis=0), sec_ref[...])
    filter_ref[...] = spec_ref[SETS * HALF :, :]
    zero = jnp.zeros((HALF, LANES), F32)
    sums = [(zero, zero) for _ in range(OWNED)]
    lines = multiplied(spec_ref, spec_ref, SETS * HALF, sums)
    for own in range(OWNED):
        sum_ref[own * HALF : (own + 1) * HALF, :] = jnp.concatenate(sums[own], axis=1)
    inv_ref[...] = mm(jnp.concatenate(lines, axis=0), secb_ref[...])
    for p in range(SETS // 2):
        res = inverse(inv_ref[2 * p * HALF : 2 * (p + 1) * HALF, :], tw_ref, last_ref)
        for u in range(2):
            keep(fin_ref, 2 * p + u, res[:, u * LANES : (u + 1) * LANES])


def conv_other_kernel(
    got_ref,
    filter_ref,
    sum_ref,
    done_ref,
    order_ref,
    back_ref,
    fs_ref,
    tw_ref,
    sec_ref,
    secb_ref,
    last_ref,
    out_ref,
    sig_ref,
    spec_ref,
    inv_ref,
    fin_ref,
):
    sort_signals(got_ref, order_ref, sig_ref)
    spec_ref[...] = mm(jnp.concatenate(forward_lines(sig_ref, fs_ref, tw_ref), axis=0), sec_ref[...])
    sums = []
    for own in range(OWNED):
        found = sum_ref[own * HALF : (own + 1) * HALF, :]
        sums.append((found[:, :LANES], found[:, LANES:]))
    lines = multiplied(spec_ref, filter_ref, 0, sums)
    lines.append(three(jnp.concatenate([jnp.concatenate(pair, axis=1) for pair in sums], axis=0)))
    inv_ref[...] = mm(jnp.concatenate(lines, axis=0), secb_ref[...])
    for p in range(SETS // 2 + 1):
        res = inverse(inv_ref[2 * p * HALF : 2 * (p + 1) * HALF, :], tw_ref, last_ref)
        for u in range(2):
            slots = [2 * p + u] if p < SETS // 2 else [SETS + u * HALVES + half for half in range(HALVES)]
            for s in slots:
                keep(fin_ref, s, res[:, u * LANES : (u + 1) * LANES])
    back = back_ref[...]
    for h in range(2):
        rows = mm(back, jnp.concatenate([done_ref[h], fin_ref[h]], axis=0)).astype(BF16)
        lo = 2 * h * TILE
        out_ref[lo : lo + TILE, :] = rows[:, :LANES]
        out_ref[lo + TILE : lo + 2 * TILE, :] = rows[:, LANES:]


def exchange(rows):
    parts = rows.reshape(rows.shape[0] // OWNED, OWNED, LANES)
    parts = lax.all_to_all(parts, ("ctx", "zh"), split_axis=0, concat_axis=0, tiled=True)
    return parts.reshape(rows.shape)


def local(query, key_input, value_input, filter_taps, grad_output):
    sort, order_own, order_other, back, first_signal, first_filter, twist, second, second_back, last = tables()
    limit = pltpu.CompilerParams(vmem_limit_bytes=32 * 1024 * 1024)
    hbm = pl.BlockSpec(memory_space=pltpu.HBM)
    near = (query, key_input, value_input, grad_output)
    inputs = (query, key_input, value_input, filter_taps, grad_output)
    rows = jax.ShapeDtypeStruct((OWNERS * CHUNK, LANES), BF16)
    sent = pl.pallas_call(
        pack_kernel,
        out_shape=rows,
        in_specs=[hbm] * 5,
        scratch_shapes=[
            pltpu.VMEM((4,) + query.shape[1:], BF16),
            pltpu.VMEM(filter_taps.shape, F32),
            pltpu.VMEM((CHUNK * HALF, PARTS * LANES), BF16),
            pltpu.SemaphoreType.DMA((5,)),
        ],
        compiler_params=limit,
        name="pack",
    )(*[pltpu.with_memory_space_constraint(x, pltpu.HBM) for x in inputs])
    got = exchange(sent)
    other = lax.ppermute(got, "core", SWAP)
    extra = OWNED * HALVES
    pair = jax.ShapeDtypeStruct((OWNED * HALF, 2 * LANES), F32)
    filter_spec, sums, done = pl.pallas_call(
        conv_own_kernel,
        out_shape=(pair, pair, jax.ShapeDtypeStruct((2, SETS * GROUP, 2 * LANES), BF16)),
        scratch_shapes=[
            pltpu.VMEM((BLOCKS, (SETS + extra) * LANES), BF16),
            pltpu.VMEM(((SETS + OWNED) * HALF, 2 * LANES), F32),
            pltpu.VMEM((SETS * HALF, 2 * LANES), F32),
        ],
        compiler_params=limit,
        cost_estimate=pl.CostEstimate(flops=2 * 10**9, bytes_accessed=4 * 10**6, transcendentals=0),
        name="conv_own",
    )(got, order_own, first_signal, first_filter, twist, second, second_back, last)
    results = pl.pallas_call(
        conv_other_kernel,
        out_shape=rows,
        scratch_shapes=[
            pltpu.VMEM((BLOCKS, SETS * LANES), BF16),
            pltpu.VMEM((SETS * HALF, 2 * LANES), F32),
            pltpu.VMEM(((SETS + OWNED) * HALF, 2 * LANES), F32),
            pltpu.VMEM((2, (SETS + extra) * GROUP, 2 * LANES), BF16),
        ],
        compiler_params=limit,
        name="conv_other",
    )(other, filter_spec, sums, done, order_other, back, first_signal, twist, second, second_back, last)
    returned = exchange(results)
    swapped = lax.ppermute(returned, "core", SWAP)
    like = jax.ShapeDtypeStruct(query.shape, BF16)
    unpack = functools.partial(
        pl.pallas_call,
        out_shape=(like, like, like, like, jax.ShapeDtypeStruct(filter_taps.shape, F32)),
        out_specs=[hbm] * 5,
        scratch_shapes=[
            pltpu.VMEM((4, C // CORES // LANES, LANES, LANES), BF16),
            pltpu.VMEM((C // CORES // LANES, LANES, LANES), F32),
            pltpu.SemaphoreType.DMA((5, C // CORES // LANES)),
        ],
        compiler_params=limit,
        cost_estimate=pl.CostEstimate(flops=10**9, bytes_accessed=2 * 10**6, transcendentals=0),
    )
    half = unpack(functools.partial(unpack_kernel, True), name="unpack_own")(*near, returned, sort)
    block = pl.BlockSpec(memory_space=pltpu.VMEM)
    return unpack(
        functools.partial(unpack_kernel, False),
        in_specs=[block] * 6 + [hbm] * 5,
        input_output_aliases={6 + i: i for i in range(5)},
        name="unpack_other",
    )(*near, swapped, sort, *half)


def solution(mesh):
    split = jax.sharding.Mesh(mesh.devices.reshape(BLOCKS, HALVES, CORES), ("ctx", "zh", "core"))
    shared = P(("zh", "core"), "ctx", None)
    taps = P("ctx", None)
    return jax.shard_map(
        local,
        mesh=split,
        in_specs=(shared, shared, shared, taps, shared),
        out_specs=(shared, shared, shared, shared, taps),
        check_vma=False,
    )
```

```python
import functools

import jax
import jax.numpy as jnp
import ml_dtypes
import numpy as np
from jax import lax
from jax.experimental import pallas as pl
from jax.experimental.pallas import tpu as pltpu
from jax.sharding import PartitionSpec as P

BF16 = jnp.bfloat16
F32 = jnp.float32

BLOCKS = 64
LANES = 128
ROWS = 128
HALF = 64
SEQS = 4
C = 512
CORES = 2
HALVES = 2
KINDS = 3
OWNERS = 128
OWNED = C // CORES // OWNERS
GROUP = 16
PARTS = 5
CHUNK = PARTS * OWNED
TILE = GROUP * HALVES * CHUNK
SWAP = ((0, 1), (1, 0))
FORWARD_PAIRS = 4
INVERSE_PAIRS = 5


def two_terms(table):
    high = table.astype(ml_dtypes.bfloat16)
    low = (table - high.astype(np.float64)).astype(ml_dtypes.bfloat16)
    return high, low


def tables():
    k1 = np.arange(HALF)[:, None] + 0.5
    angle1 = 2.0 * np.pi * k1 * np.arange(BLOCKS)[None, :] / ROWS
    first = np.concatenate([np.cos(angle1), -np.sin(angle1)], axis=0)
    first_high, first_low = two_terms(first)
    first_signal = np.concatenate([first_high, first_low], axis=1)
    first_filter = np.concatenate([first_high, first_low, first_high], axis=1)
    angle_t = 2.0 * np.pi * k1 * np.arange(LANES)[None, :] / (ROWS * LANES)
    twist = np.concatenate([np.cos(angle_t), -np.sin(angle_t)], axis=0).astype(np.float32)
    index = np.arange(LANES)
    angle2 = 2.0 * np.pi * ((index[:, None] * index[None, :]) % LANES) / LANES
    cos2, sin2 = np.cos(angle2), np.sin(angle2)
    second = np.block([[cos2, -sin2], [sin2, cos2]])
    second_back = np.block([[cos2, sin2], [-sin2, cos2]])
    last = np.concatenate([np.cos(angle1.T), -np.sin(angle1.T)], axis=1) * (2.0 / (ROWS * LANES))
    last_high, last_low = two_terms(last)
    last_stack = np.concatenate([last_high, last_high, last_low], axis=1)
    line = np.arange(TILE)
    half = line % (HALVES * CHUNK) // CHUNK
    part = line % CHUNK // OWNED
    own = line % OWNED
    slot = np.where(
        part == 4, 2 * OWNED * SEQS + own * HALVES + half, (part % 2 * OWNED + own) * SEQS + half * CORES + part // 2
    )
    order = np.zeros((TILE, TILE))
    order[slot * GROUP + line // (HALVES * CHUNK), line] = 1.0
    row = np.arange(CHUNK * HALF)
    own = OWNED * (row // CHUNK) + row % OWNED
    part = row % CHUNK // OWNED
    sort = np.zeros((CORES, CHUNK * HALF, KINDS * LANES))
    for whose in range(CORES):
        for kind, wanted in enumerate((2 * whose, 2 * whose + 1, 4)):
            sort[whose, row[part == wanted], kind * LANES + own[part == wanted]] = 1.0
    high, low = two_terms(second)
    back_high, back_low = two_terms(second_back)
    return (
        sort.astype(ml_dtypes.bfloat16),
        order.astype(ml_dtypes.bfloat16),
        np.ascontiguousarray(order.T).astype(ml_dtypes.bfloat16),
        first_signal,
        first_filter,
        twist,
        np.concatenate([high, high, low], axis=0),
        np.concatenate([back_high, back_high, back_low], axis=0),
        last_stack,
    )


def mm(a, b, dims=((1,), (0,))):
    return lax.dot_general(a, b, (dims, ((), ())), preferred_element_type=F32)


def columns(core, b):
    return pl.ds(pl.multiple_of(core * (C // CORES) + b * LANES, LANES), LANES)


def gate_kernel(q_hbm, k_hbm, v_hbm, g_hbm, out_ref, pick_ref, in_ref, sems):
    copies = [pltpu.make_async_copy(src.at[0], in_ref.at[i], sems.at[i]) for i, src in enumerate((k_hbm, v_hbm, g_hbm, q_hbm))]
    for copy in copies:
        copy.start()
    row = lax.broadcasted_iota(jnp.int32, (CHUNK * HALF, LANES), 0)
    lane = lax.broadcasted_iota(jnp.int32, (CHUNK * HALF, LANES), 1)
    first = (lane >> 1) * CHUNK + (lane & 1)
    for part in range(PARTS):
        chosen = jnp.where(row == first + OWNED * part, 1.0, 0.0)
        pick_ref[:, part * LANES : (part + 1) * LANES] = chosen.astype(BF16)
    for i in range(2):
        copies[2 * i].wait()
        copies[2 * i + 1].wait()
        out_ref[i] = (in_ref[2 * i].astype(F32) * in_ref[2 * i + 1].astype(F32)).astype(BF16)


def pack_kernel(gated_ref, q_ref, k_ref, v_ref, g_ref, f_ref, pick_ref, out_ref):
    core = lax.axis_index("core")
    term = lax.axis_index("zh")
    for b in range(C // CORES // LANES):
        cols = columns(core, b)
        product = (k_ref[0, :, cols].astype(F32) * v_ref[0, :, cols].astype(F32)).astype(BF16)
        grad_mix = (g_ref[0, :, cols].astype(F32) * q_ref[0, :, cols].astype(F32)).astype(BF16)
        taps = f_ref[:, cols]
        high = taps.astype(BF16).astype(F32)
        part = jnp.where(term == 0, high, taps - high).astype(BF16)
        data = [gated_ref[0, :, cols], gated_ref[1, :, cols], product, grad_mix, part]
        rows = mm(pick_ref[...], jnp.concatenate(data, axis=1), ((1,), (1,)))
        out_ref[b * CHUNK * HALF : (b + 1) * CHUNK * HALF, :] = rows.astype(BF16)


def unpack_kernel(own, q_ref, k_ref, v_ref, g_ref, got_ref, sort_ref, *refs):
    o_hbm, gq_hbm, gk_hbm, gv_hbm, gf_hbm, rows_ref, taps_ref, sems = refs[-8:]
    core = lax.axis_index("core")
    owners = core if own else 1 - core
    copies = []
    for b in range(C // CORES // LANES):
        cols = columns(owners, b)
        got = got_ref[b * CHUNK * HALF : (b + 1) * CHUNK * HALF, :]
        data = mm(got, sort_ref[0 if own else 1], ((0,), (0,)))
        mixed, back = data[:, :LANES], data[:, LANES : 2 * LANES]
        taps_ref[b] = data[:, 2 * LANES :]
        rows_ref[0, b] = (q_ref[0, :, cols].astype(F32) * mixed).astype(BF16)
        rows_ref[1, b] = (g_ref[0, :, cols].astype(F32) * mixed).astype(BF16)
        rows_ref[2, b] = (back * v_ref[0, :, cols].astype(F32)).astype(BF16)
        rows_ref[3, b] = (back * k_ref[0, :, cols].astype(F32)).astype(BF16)
        for j, out in enumerate((o_hbm, gq_hbm, gk_hbm, gv_hbm)):
            copies.append(pltpu.make_async_copy(rows_ref.at[j, b], out.at[0, :, cols], sems.at[j, b]))
        copies.append(pltpu.make_async_copy(taps_ref.at[b], gf_hbm.at[:, cols], sems.at[4, b]))
        for copy in copies[-5:]:
            copy.start()
    for copy in copies:
        copy.wait()


def split(x):
    high = x.astype(BF16)
    low = (x - high.astype(F32)).astype(BF16)
    return high, low


def multiply(lines, size, table_ref, to_ref):
    for at in range(0, len(lines), size):
        part = lines[at : at + size]
        to_ref[2 * at * HALF : 2 * (at + len(part)) * HALF, :] = mm(jnp.concatenate(part, axis=0), table_ref[...])


def conv_kernel(
    got_ref,
    order_ref,
    back_ref,
    fs_ref,
    ff_ref,
    tw_ref,
    sec_ref,
    secb_ref,
    last_ref,
    out_ref,
    sig_ref,
    spec_ref,
    inv_ref,
    fin_ref,
):
    order = order_ref[...]
    for h in range(2):
        lo = 2 * h * TILE
        data = jnp.concatenate([got_ref[lo : lo + TILE, :], got_ref[lo + TILE : lo + 2 * TILE, :]], axis=1)
        sorted_rows = mm(order, data).astype(BF16)
        for s in range(HALVES * CHUNK):
            for u in range(2):
                at = (2 * h + u) * GROUP
                sig_ref[at : at + GROUP, s * LANES : (s + 1) * LANES] = sorted_rows[
                    s * GROUP : (s + 1) * GROUP, u * LANES : (u + 1) * LANES
                ]

    def sig(s):
        return sig_ref[:, s * LANES : (s + 1) * LANES]

    wr = tw_ref[:HALF, :]
    wi = tw_ref[HALF:, :]

    def three(x):
        high, low = split(x)
        return jnp.concatenate([high, low, high], axis=1)

    def turned(first):
        halves = []
        for u in range(2):
            ar = first[:HALF, u * LANES : (u + 1) * LANES]
            ai = first[HALF:, u * LANES : (u + 1) * LANES]
            halves.append(jnp.concatenate([ar * wr - ai * wi, ar * wi + ai * wr], axis=1))
        return three(jnp.concatenate(halves, axis=0))

    base = 2 * OWNED * SEQS
    lines = []
    for p in range(OWNED * SEQS):
        data = sig_ref[:, 2 * p * LANES : 2 * (p + 1) * LANES]
        lines.append(turned(mm(fs_ref[...], jnp.concatenate([data, data], axis=0))))
    terms = [jnp.concatenate([sig(base + own * HALVES + term) for own in range(OWNED)], axis=1) for term in range(2)]
    lines.append(turned(mm(ff_ref[...], jnp.concatenate([terms[0], terms[0], terms[1]], axis=0))))
    multiply(lines, FORWARD_PAIRS, sec_ref, spec_ref)

    def inverse(full):
        cols = []
        for u in range(2):
            br = full[u * HALF : (u + 1) * HALF, :LANES]
            bi = full[u * HALF : (u + 1) * HALF, LANES:]
            cols.append(jnp.concatenate([br * wr + bi * wi, bi * wr - br * wi], axis=0))
        high, low = split(jnp.concatenate(cols, axis=1))
        return mm(last_ref[...], jnp.concatenate([high, low, high], axis=0))

    def keep(s, values):
        values = values.astype(BF16)
        for b in range(BLOCKS // GROUP):
            fin_ref[b // 2, s * GROUP : (s + 1) * GROUP, (b % 2) * LANES : (b % 2 + 1) * LANES] = values[
                b * GROUP : (b + 1) * GROUP, :
            ]

    taps, lines, places = [], [], []
    for own in range(OWNED):
        at = (base + own) * HALF
        hr = spec_ref[at : at + HALF, :LANES]
        hi = spec_ref[at : at + HALF, LANES:]
        qr = jnp.zeros((HALF, LANES), F32)
        qi = jnp.zeros((HALF, LANES), F32)
        for half in range(HALVES):
            mixed_pair, back_pair = [], []
            for u in range(CORES):
                s = own * SEQS + half * CORES + u
                pr = spec_ref[s * HALF : (s + 1) * HALF, :LANES]
                pi = spec_ref[s * HALF : (s + 1) * HALF, LANES:]
                z = OWNED * SEQS + s
                gr = spec_ref[z * HALF : (z + 1) * HALF, :LANES]
                gi = spec_ref[z * HALF : (z + 1) * HALF, LANES:]
                mixed_pair.append(jnp.concatenate([hr * pr - hi * pi, hr * pi + hi * pr], axis=1))
                back_pair.append(jnp.concatenate([gr * hr + gi * hi, gi * hr - gr * hi], axis=1))
                qr = qr + (gr * pr + gi * pi)
                qi = qi + (gi * pr - gr * pi)
            for kind, pair in ((0, mixed_pair), (1, back_pair)):
                lines.append(three(jnp.concatenate(pair, axis=0)))
                s = (kind * OWNED + own) * SEQS + half * CORES
                places.append([(s,), (s + 1,)])
        taps.append(jnp.concatenate([qr, qi], axis=1))
    lines.append(three(jnp.concatenate(taps, axis=0)))
    places.append([[base + own * HALVES + half for half in range(HALVES)] for own in range(OWNED)])
    multiply(lines, INVERSE_PAIRS, secb_ref, inv_ref)
    for p, pair in enumerate(places):
        res = inverse(inv_ref[2 * p * HALF : 2 * (p + 1) * HALF, :])
        for u in range(2):
            for s in pair[u]:
                keep(s, res[:, u * LANES : (u + 1) * LANES])

    back = back_ref[...]
    for h in range(2):
        rows = mm(back, fin_ref[h]).astype(BF16)
        lo = 2 * h * TILE
        out_ref[lo : lo + TILE, :] = rows[:, :LANES]
        out_ref[lo + TILE : lo + 2 * TILE, :] = rows[:, LANES:]


def exchange(rows):
    parts = rows.reshape(rows.shape[0] // OWNED, OWNED, LANES)
    parts = lax.all_to_all(parts, ("ctx", "zh"), split_axis=0, concat_axis=0, tiled=True)
    return parts.reshape(rows.shape)


def local(query, key_input, value_input, filter_taps, grad_output):
    sort, order, back, first_signal, first_filter, twist, second, second_back, last = tables()
    limit = pltpu.CompilerParams(vmem_limit_bytes=32 * 1024 * 1024)
    hbm = pl.BlockSpec(memory_space=pltpu.HBM)
    near = (query, key_input, value_input, grad_output)
    other = [lax.ppermute(x, "core", SWAP) for x in near]
    rows = jax.ShapeDtypeStruct((OWNERS * CHUNK, LANES), BF16)
    gated, pick = pl.pallas_call(
        gate_kernel,
        out_shape=(
            jax.ShapeDtypeStruct((2,) + query.shape[1:], BF16),
            jax.ShapeDtypeStruct((CHUNK * HALF, PARTS * LANES), BF16),
        ),
        in_specs=[hbm] * 4,
        scratch_shapes=[pltpu.VMEM((4,) + query.shape[1:], BF16), pltpu.SemaphoreType.DMA((4,))],
        compiler_params=limit,
        cost_estimate=pl.CostEstimate(flops=10**9, bytes_accessed=2 * 10**6, transcendentals=0),
        name="gate",
    )(*[pltpu.with_memory_space_constraint(x, pltpu.HBM) for x in near])
    sent = pl.pallas_call(pack_kernel, out_shape=rows, compiler_params=limit, name="pack")(gated, *other, filter_taps, pick)
    got = exchange(sent)
    signals = (KINDS - 1) * OWNED * SEQS + OWNED
    results = pl.pallas_call(
        conv_kernel,
        out_shape=rows,
        scratch_shapes=[
            pltpu.VMEM((BLOCKS, HALVES * CHUNK * LANES), BF16),
            pltpu.VMEM((signals * HALF, 2 * LANES), F32),
            pltpu.VMEM((signals * HALF, 2 * LANES), F32),
            pltpu.VMEM((2, TILE, 2 * LANES), BF16),
        ],
        compiler_params=limit,
        name="conv",
    )(got, order, back, first_signal, first_filter, twist, second, second_back, last)
    returned = exchange(results)
    swapped = lax.ppermute(returned, "core", SWAP)
    like = jax.ShapeDtypeStruct(query.shape, BF16)
    unpack = functools.partial(
        pl.pallas_call,
        out_shape=(like, like, like, like, jax.ShapeDtypeStruct(filter_taps.shape, F32)),
        out_specs=[hbm] * 5,
        scratch_shapes=[
            pltpu.VMEM((4, C // CORES // LANES, LANES, LANES), BF16),
            pltpu.VMEM((C // CORES // LANES, LANES, LANES), F32),
            pltpu.SemaphoreType.DMA((5, C // CORES // LANES)),
        ],
        compiler_params=limit,
        cost_estimate=pl.CostEstimate(flops=10**9, bytes_accessed=2 * 10**6, transcendentals=0),
    )
    half = unpack(functools.partial(unpack_kernel, True), name="unpack_own")(*near, returned, sort)
    block = pl.BlockSpec(memory_space=pltpu.VMEM)
    return unpack(
        functools.partial(unpack_kernel, False),
        in_specs=[block] * 6 + [hbm] * 5,
        input_output_aliases={6 + i: i for i in range(5)},
        name="unpack_other",
    )(*near, swapped, sort, *half)


def solution(mesh):
    split = jax.sharding.Mesh(mesh.devices.reshape(BLOCKS, HALVES, CORES), ("ctx", "zh", "core"))
    shared = P(("zh", "core"), "ctx", None)
    taps = P("ctx", None)
    return jax.shard_map(
        local,
        mesh=split,
        in_specs=(shared, shared, shared, taps, shared),
        out_specs=(shared, shared, shared, shared, taps),
        check_vma=False,
    )
```

```python
import functools

import jax
import jax.numpy as jnp
import ml_dtypes
import numpy as np
from jax import lax
from jax.experimental import pallas as pl
from jax.experimental.pallas import tpu as pltpu
from jax.sharding import PartitionSpec as P

BF16 = jnp.bfloat16
F32 = jnp.float32

BLOCKS = 64
LANES = 128
ROWS = 128
HALF = 64
SEQS = 4
C = 512
CORES = 2
HALVES = 2
KINDS = 3
OWNERS = 128
OWNED = C // CORES // OWNERS
GROUP = 16
PARTS = 5
CHUNK = PARTS * OWNED
TILE = GROUP * HALVES * CHUNK
SETS = 2 * OWNED * HALVES
SWAP = ((0, 1), (1, 0))


def two_terms(table):
    high = table.astype(ml_dtypes.bfloat16)
    low = (table - high.astype(np.float64)).astype(ml_dtypes.bfloat16)
    return high, low


def tables():
    k1 = np.arange(HALF)[:, None] + 0.5
    angle1 = 2.0 * np.pi * k1 * np.arange(BLOCKS)[None, :] / ROWS
    first = np.concatenate([np.cos(angle1), -np.sin(angle1)], axis=0)
    first_high, first_low = two_terms(first)
    first_signal = np.concatenate([first_high, first_low], axis=1)
    first_filter = np.concatenate([first_high, first_low, first_high], axis=1)
    angle_t = 2.0 * np.pi * k1 * np.arange(LANES)[None, :] / (ROWS * LANES)
    twist = np.concatenate([np.cos(angle_t), -np.sin(angle_t)], axis=0).astype(np.float32)
    index = np.arange(LANES)
    angle2 = 2.0 * np.pi * ((index[:, None] * index[None, :]) % LANES) / LANES
    cos2, sin2 = np.cos(angle2), np.sin(angle2)
    second = np.block([[cos2, -sin2], [sin2, cos2]])
    second_back = np.block([[cos2, sin2], [-sin2, cos2]])
    last = np.concatenate([np.cos(angle1.T), -np.sin(angle1.T)], axis=1) * (2.0 / (ROWS * LANES))
    last_high, last_low = two_terms(last)
    last_stack = np.concatenate([last_high, last_high, last_low], axis=1)
    line = np.arange(TILE)
    block = line // (HALVES * CHUNK)
    half = line % (HALVES * CHUNK) // CHUNK
    part = line % CHUNK // OWNED
    own = line % OWNED
    slot = ((part % 2 * OWNED + own) * HALVES + half) * GROUP + block
    last_slot = (own * HALVES + half) * GROUP + block
    order_own = np.zeros((SETS * GROUP + OWNED * HALVES * GROUP, TILE))
    order_other = np.zeros((SETS * GROUP, TILE))
    order_own[slot[part < 2], line[part < 2]] = 1.0
    order_own[SETS * GROUP + last_slot[part == 4], line[part == 4]] = 1.0
    chosen = (part == 2) | (part == 3)
    order_other[slot[chosen], line[chosen]] = 1.0
    back = np.zeros((TILE, TILE))
    back[line, np.where(part == 4, 2 * SETS * GROUP + last_slot, part // 2 * SETS * GROUP + slot)] = 1.0
    row = np.arange(CHUNK * HALF)
    own = OWNED * (row // CHUNK) + row % OWNED
    part = row % CHUNK // OWNED
    sort = np.zeros((CORES, CHUNK * HALF, KINDS * LANES))
    for whose in range(CORES):
        for kind, wanted in enumerate((2 * whose, 2 * whose + 1, 4)):
            sort[whose, row[part == wanted], kind * LANES + own[part == wanted]] = 1.0
    high, low = two_terms(second)
    back_high, back_low = two_terms(second_back)
    return (
        sort.astype(ml_dtypes.bfloat16),
        order_own.astype(ml_dtypes.bfloat16),
        order_other.astype(ml_dtypes.bfloat16),
        back.astype(ml_dtypes.bfloat16),
        first_signal,
        first_filter,
        twist,
        np.concatenate([high, high, low], axis=0),
        np.concatenate([back_high, back_high, back_low], axis=0),
        last_stack,
    )


def mm(a, b, dims=((1,), (0,))):
    return lax.dot_general(a, b, (dims, ((), ())), preferred_element_type=F32)


def columns(core, b):
    return pl.ds(pl.multiple_of(core * (C // CORES) + b * LANES, LANES), LANES)


def pack_kernel(q_hbm, k_hbm, v_hbm, f_hbm, g_hbm, out_ref, in_ref, f_ref, pick_ref, sems):
    copies = [pltpu.make_async_copy(src.at[0], in_ref.at[i], sems.at[i]) for i, src in enumerate((k_hbm, v_hbm, g_hbm, q_hbm))]
    copies.append(pltpu.make_async_copy(f_hbm, f_ref, sems.at[4]))
    for copy in copies:
        copy.start()
    core = lax.axis_index("core")
    term = lax.axis_index("zh")
    row = lax.broadcasted_iota(jnp.int32, (CHUNK * HALF, LANES), 0)
    lane = lax.broadcasted_iota(jnp.int32, (CHUNK * HALF, LANES), 1)
    first = (lane >> 1) * CHUNK + (lane & 1)
    for part in range(PARTS):
        chosen = jnp.where(row == first + OWNED * part, 1.0, 0.0)
        pick_ref[:, part * LANES : (part + 1) * LANES] = chosen.astype(BF16)
    for copy in copies:
        copy.wait()
    for b in range(C // CORES // LANES):
        data = []
        for owners in (core, 1 - core):
            cols = columns(owners, b)
            for i in (0, 2):
                data.append((in_ref[i, :, cols].astype(F32) * in_ref[i + 1, :, cols].astype(F32)).astype(BF16))
        taps = f_ref[:, columns(core, b)]
        high = taps.astype(BF16).astype(F32)
        data.append(jnp.where(term == 0, high, taps - high).astype(BF16))
        rows = mm(pick_ref[...], jnp.concatenate(data, axis=1), ((1,), (1,)))
        out_ref[b * CHUNK * HALF : (b + 1) * CHUNK * HALF, :] = rows.astype(BF16)


def unpack_kernel(own, q_ref, k_ref, v_ref, g_ref, got_ref, sort_ref, *refs):
    o_hbm, gq_hbm, gk_hbm, gv_hbm, gf_hbm, rows_ref, taps_ref, sems = refs[-8:]
    core = lax.axis_index("core")
    owners = core if own else 1 - core
    copies = []
    for b in range(C // CORES // LANES):
        cols = columns(owners, b)
        got = got_ref[b * CHUNK * HALF : (b + 1) * CHUNK * HALF, :]
        data = mm(got, sort_ref[0 if own else 1], ((0,), (0,)))
        mixed, back = data[:, :LANES], data[:, LANES : 2 * LANES]
        taps_ref[b] = data[:, 2 * LANES :]
        rows_ref[0, b] = (q_ref[0, :, cols].astype(F32) * mixed).astype(BF16)
        rows_ref[1, b] = (g_ref[0, :, cols].astype(F32) * mixed).astype(BF16)
        rows_ref[2, b] = (back * v_ref[0, :, cols].astype(F32)).astype(BF16)
        rows_ref[3, b] = (back * k_ref[0, :, cols].astype(F32)).astype(BF16)
        for j, out in enumerate((o_hbm, gq_hbm, gk_hbm, gv_hbm)):
            copies.append(pltpu.make_async_copy(rows_ref.at[j, b], out.at[0, :, cols], sems.at[j, b]))
        copies.append(pltpu.make_async_copy(taps_ref.at[b], gf_hbm.at[:, cols], sems.at[4, b]))
        for copy in copies[-5:]:
            copy.start()
    for copy in copies:
        copy.wait()


def split(x):
    high = x.astype(BF16)
    low = (x - high.astype(F32)).astype(BF16)
    return high, low


def three(x):
    high, low = split(x)
    return jnp.concatenate([high, low, high], axis=1)


def multiply(lines, size, table_ref, to_ref):
    for at in range(0, len(lines), size):
        part = lines[at : at + size]
        to_ref[2 * at * HALF : 2 * (at + len(part)) * HALF, :] = mm(jnp.concatenate(part, axis=0), table_ref[...])


def sort_signals(got_ref, order_ref, sig_ref):
    order = order_ref[...]
    for h in range(2):
        lo = 2 * h * TILE
        data = jnp.concatenate([got_ref[lo : lo + TILE, :], got_ref[lo + TILE : lo + 2 * TILE, :]], axis=1)
        sorted_rows = mm(order, data).astype(BF16)
        for s in range(order.shape[0] // GROUP):
            for u in range(2):
                at = (2 * h + u) * GROUP
                sig_ref[at : at + GROUP, s * LANES : (s + 1) * LANES] = sorted_rows[
                    s * GROUP : (s + 1) * GROUP, u * LANES : (u + 1) * LANES
                ]


def turned(first, tw_ref):
    wr, wi = tw_ref[:HALF, :], tw_ref[HALF:, :]
    halves = []
    for u in range(2):
        ar = first[:HALF, u * LANES : (u + 1) * LANES]
        ai = first[HALF:, u * LANES : (u + 1) * LANES]
        halves.append(jnp.concatenate([ar * wr - ai * wi, ar * wi + ai * wr], axis=1))
    return three(jnp.concatenate(halves, axis=0))


def forward_lines(sig_ref, fs_ref, tw_ref):
    lines = []
    for p in range(SETS // 2):
        data = sig_ref[:, 2 * p * LANES : 2 * (p + 1) * LANES]
        lines.append(turned(mm(fs_ref[...], jnp.concatenate([data, data], axis=0)), tw_ref))
    return lines


def multiplied(spec_ref, filter_ref, at, sums):
    lines = []
    for own in range(OWNED):
        hr = filter_ref[at + own * HALF : at + (own + 1) * HALF, :LANES]
        hi = filter_ref[at + own * HALF : at + (own + 1) * HALF, LANES:]
        mixed_pair, back_pair = [], []
        qr, qi = sums[own]
        for half in range(HALVES):
            s = own * HALVES + half
            z = OWNED * HALVES + s
            pr = spec_ref[s * HALF : (s + 1) * HALF, :LANES]
            pi = spec_ref[s * HALF : (s + 1) * HALF, LANES:]
            gr = spec_ref[z * HALF : (z + 1) * HALF, :LANES]
            gi = spec_ref[z * HALF : (z + 1) * HALF, LANES:]
            mixed_pair.append(jnp.concatenate([hr * pr - hi * pi, hr * pi + hi * pr], axis=1))
            back_pair.append(jnp.concatenate([gr * hr + gi * hi, gi * hr - gr * hi], axis=1))
            qr = qr + (gr * pr + gi * pi)
            qi = qi + (gi * pr - gr * pi)
        sums[own] = (qr, qi)
        lines.append((own, three(jnp.concatenate(mixed_pair, axis=0))))
        lines.append((OWNED + own, three(jnp.concatenate(back_pair, axis=0))))
    return [line for _, line in sorted(lines, key=lambda entry: entry[0])]


def inverse(full, tw_ref, last_ref):
    wr, wi = tw_ref[:HALF, :], tw_ref[HALF:, :]
    cols = []
    for u in range(2):
        br = full[u * HALF : (u + 1) * HALF, :LANES]
        bi = full[u * HALF : (u + 1) * HALF, LANES:]
        cols.append(jnp.concatenate([br * wr + bi * wi, bi * wr - br * wi], axis=0))
    high, low = split(jnp.concatenate(cols, axis=1))
    return mm(last_ref[...], jnp.concatenate([high, low, high], axis=0))


def keep(fin_ref, s, values):
    values = values.astype(BF16)
    for b in range(BLOCKS // GROUP):
        fin_ref[b // 2, s * GROUP : (s + 1) * GROUP, (b % 2) * LANES : (b % 2 + 1) * LANES] = values[
            b * GROUP : (b + 1) * GROUP, :
        ]


def conv_own_kernel(
    got_ref, order_ref, fs_ref, ff_ref, tw_ref, sec_ref, secb_ref, last_ref, filter_ref, sum_ref, fin_ref, sig_ref, spec_ref, inv_ref
):
    sort_signals(got_ref, order_ref, sig_ref)
    lines = forward_lines(sig_ref, fs_ref, tw_ref)
    terms = []
    for term in range(HALVES):
        places = [SETS * LANES + (own * HALVES + term) * LANES for own in range(OWNED)]
        terms.append(jnp.concatenate([sig_ref[:, at : at + LANES] for at in places], axis=1))
    lines.append(turned(mm(ff_ref[...], jnp.concatenate([terms[0], terms[0], terms[1]], axis=0)), tw_ref))
    multiply(lines, 3, sec_ref, spec_ref)
    filter_ref[...] = spec_ref[SETS * HALF :, :]
    zero = jnp.zeros((HALF, LANES), F32)
    sums = [(zero, zero) for _ in range(OWNED)]
    lines = multiplied(spec_ref, spec_ref, SETS * HALF, sums)
    for own in range(OWNED):
        sum_ref[own * HALF : (own + 1) * HALF, :] = jnp.concatenate(sums[own], axis=1)
    multiply(lines, 2, secb_ref, inv_ref)
    for p in range(SETS // 2):
        res = inverse(inv_ref[2 * p * HALF : 2 * (p + 1) * HALF, :], tw_ref, last_ref)
        for u in range(2):
            keep(fin_ref, 2 * p + u, res[:, u * LANES : (u + 1) * LANES])


def conv_other_kernel(
    got_ref,
    filter_ref,
    sum_ref,
    done_ref,
    order_ref,
    back_ref,
    fs_ref,
    tw_ref,
    sec_ref,
    secb_ref,
    last_ref,
    out_ref,
    sig_ref,
    spec_ref,
    inv_ref,
    fin_ref,
):
    sort_signals(got_ref, order_ref, sig_ref)
    multiply(forward_lines(sig_ref, fs_ref, tw_ref), 2, sec_ref, spec_ref)
    sums = []
    for own in range(OWNED):
        found = sum_ref[own * HALF : (own + 1) * HALF, :]
        sums.append((found[:, :LANES], found[:, LANES:]))
    lines = multiplied(spec_ref, filter_ref, 0, sums)
    lines.append(three(jnp.concatenate([jnp.concatenate(pair, axis=1) for pair in sums], axis=0)))
    multiply(lines, 3, secb_ref, inv_ref)
    for p in range(SETS // 2 + 1):
        res = inverse(inv_ref[2 * p * HALF : 2 * (p + 1) * HALF, :], tw_ref, last_ref)
        for u in range(2):
            slots = [2 * p + u] if p < SETS // 2 else [SETS + u * HALVES + half for half in range(HALVES)]
            for s in slots:
                keep(fin_ref, s, res[:, u * LANES : (u + 1) * LANES])
    back = back_ref[...]
    for h in range(2):
        rows = mm(back, jnp.concatenate([done_ref[h], fin_ref[h]], axis=0)).astype(BF16)
        lo = 2 * h * TILE
        out_ref[lo : lo + TILE, :] = rows[:, :LANES]
        out_ref[lo + TILE : lo + 2 * TILE, :] = rows[:, LANES:]


def exchange(rows):
    parts = rows.reshape(rows.shape[0] // OWNED, OWNED, LANES)
    parts = lax.all_to_all(parts, ("ctx", "zh"), split_axis=0, concat_axis=0, tiled=True)
    return parts.reshape(rows.shape)


def local(query, key_input, value_input, filter_taps, grad_output):
    sort, order_own, order_other, back, first_signal, first_filter, twist, second, second_back, last = tables()
    limit = pltpu.CompilerParams(vmem_limit_bytes=32 * 1024 * 1024)
    hbm = pl.BlockSpec(memory_space=pltpu.HBM)
    near = (query, key_input, value_input, grad_output)
    inputs = (query, key_input, value_input, filter_taps, grad_output)
    rows = jax.ShapeDtypeStruct((OWNERS * CHUNK, LANES), BF16)
    sent = pl.pallas_call(
        pack_kernel,
        out_shape=rows,
        in_specs=[hbm] * 5,
        scratch_shapes=[
            pltpu.VMEM((4,) + query.shape[1:], BF16),
            pltpu.VMEM(filter_taps.shape, F32),
            pltpu.VMEM((CHUNK * HALF, PARTS * LANES), BF16),
            pltpu.SemaphoreType.DMA((5,)),
        ],
        compiler_params=limit,
        name="pack",
    )(*[pltpu.with_memory_space_constraint(x, pltpu.HBM) for x in inputs])
    got = exchange(sent)
    other = lax.ppermute(got, "core", SWAP)
    extra = OWNED * HALVES
    pair = jax.ShapeDtypeStruct((OWNED * HALF, 2 * LANES), F32)
    filter_spec, sums, done = pl.pallas_call(
        conv_own_kernel,
        out_shape=(pair, pair, jax.ShapeDtypeStruct((2, SETS * GROUP, 2 * LANES), BF16)),
        scratch_shapes=[
            pltpu.VMEM((BLOCKS, (SETS + extra) * LANES), BF16),
            pltpu.VMEM(((SETS + OWNED) * HALF, 2 * LANES), F32),
            pltpu.VMEM((SETS * HALF, 2 * LANES), F32),
        ],
        compiler_params=limit,
        cost_estimate=pl.CostEstimate(flops=2 * 10**9, bytes_accessed=4 * 10**6, transcendentals=0),
        name="conv_own",
    )(got, order_own, first_signal, first_filter, twist, second, second_back, last)
    results = pl.pallas_call(
        conv_other_kernel,
        out_shape=rows,
        scratch_shapes=[
            pltpu.VMEM((BLOCKS, SETS * LANES), BF16),
            pltpu.VMEM((SETS * HALF, 2 * LANES), F32),
            pltpu.VMEM(((SETS + OWNED) * HALF, 2 * LANES), F32),
            pltpu.VMEM((2, (SETS + extra) * GROUP, 2 * LANES), BF16),
        ],
        compiler_params=limit,
        name="conv_other",
    )(other, filter_spec, sums, done, order_other, back, first_signal, twist, second, second_back, last)
    returned = exchange(results)
    swapped = lax.ppermute(returned, "core", SWAP)
    like = jax.ShapeDtypeStruct(query.shape, BF16)
    unpack = functools.partial(
        pl.pallas_call,
        out_shape=(like, like, like, like, jax.ShapeDtypeStruct(filter_taps.shape, F32)),
        out_specs=[hbm] * 5,
        scratch_shapes=[
            pltpu.VMEM((4, C // CORES // LANES, LANES, LANES), BF16),
            pltpu.VMEM((C // CORES // LANES, LANES, LANES), F32),
            pltpu.SemaphoreType.DMA((5, C // CORES // LANES)),
        ],
        compiler_params=limit,
        cost_estimate=pl.CostEstimate(flops=10**9, bytes_accessed=2 * 10**6, transcendentals=0),
    )
    half = unpack(functools.partial(unpack_kernel, True), name="unpack_own")(*near, returned, sort)
    block = pl.BlockSpec(memory_space=pltpu.VMEM)
    return unpack(
        functools.partial(unpack_kernel, False),
        in_specs=[block] * 6 + [hbm] * 5,
        input_output_aliases={6 + i: i for i in range(5)},
        name="unpack_other",
    )(*near, swapped, sort, *half)


def solution(mesh):
    split = jax.sharding.Mesh(mesh.devices.reshape(BLOCKS, HALVES, CORES), ("ctx", "zh", "core"))
    shared = P(("zh", "core"), "ctx", None)
    taps = P("ctx", None)
    return jax.shard_map(
        local,
        mesh=split,
        in_specs=(shared, shared, shared, taps, shared),
        out_specs=(shared, shared, shared, shared, taps),
        check_vma=False,
    )
```
